32 devices in a mesh: dp: 16 (over z, y, x), seq: 2 (over core).
Axes of the slice: x: 2, y: 2, z: 4, core: 2. Of those that a mesh axis runs over, the one named last changes fastest.
Arguments:
- hidden_in: bfloat16 [16, 1024, 1408], P('dp', 'seq'), may hold values from -6 to 6
- skip_in: bfloat16 [16, 1024, 1408], P('dp', 'seq'), may hold values from -6 to 6
- text: bfloat16 [16, 333, 1024], P('dp'), may hold values from -6 to 6
- temb: float32 [16, 1408], P('dp'), may hold values from -6 to 6
- mt5_len: int32 [16], P('dp'), may hold values from 10 to 256, as said below
- cotangent: bfloat16 [16, 1024, 1408], P('dp', 'seq'), may hold values from -6 to 6
- skip_w: bfloat16 [2816, 1408], P(('dp', 'seq')), may hold values from -0.109375 to 0.109375
- time_w: bfloat16 [1408, 1408], P(('dp', 'seq')), may hold values from -0.15625 to 0.15625
- qkv_w: bfloat16 [1408, 4224], P(('dp', 'seq')), may hold values from -0.15625 to 0.15625
- out_w: bfloat16 [1408, 1408], P(('dp', 'seq')), may hold values from -0.625 to 0.625
- q2_w: bfloat16 [1408, 1408], P(('dp', 'seq')), may hold values from -0.15625 to 0.15625
- kv2_w: bfloat16 [1024, 2816], P(('dp', 'seq')), may hold values from -0.1875 to 0.1875
- out2_w: bfloat16 [1408, 1408], P(('dp', 'seq')), may hold values from -0.375 to 0.375
- fc1_w: bfloat16 [1408, 6144], P(('dp', 'seq')), may hold values from -0.15625 to 0.15625
- fc2_w: bfloat16 [6144, 1408], P(None, ('dp', 'seq')), may hold values from -0.078125 to 0.078125
- vectors: bfloat16 [19, 1408], P(None, ('dp', 'seq'))
- head_norms: bfloat16 [8, 88], replicated
- fc_bias: bfloat16 [6144], replicated, may hold values from -3 to 3
Outputs:
- block_out: float32 [16, 1024, 1408], P('dp', 'seq')
- grad_hidden: float32 [16, 1024, 1408], P('dp', 'seq')
- grad_skip: float32 [16, 1024, 1408], P('dp', 'seq')
- grad_text: float32 [16, 333, 1024], P('dp')
- grad_temb: float32 [16, 1408], P('dp')
- grad_skip_w: float32 [2816, 1408], P(('dp', 'seq'))
- grad_time_w: float32 [1408, 1408], P(('dp', 'seq'))
- grad_qkv_w: float32 [1408, 4224], P(('dp', 'seq'))
- grad_out_w: float32 [1408, 1408], P(('dp', 'seq'))
- grad_q2_w: float32 [1408, 1408], P(('dp', 'seq'))
- grad_kv2_w: float32 [1024, 2816], P(('dp', 'seq'))
- grad_out2_w: float32 [1408, 1408], P(('dp', 'seq'))
- grad_fc1_w: float32 [1408, 6144], P(('dp', 'seq'))
- grad_fc2_w: float32 [6144, 1408], P(None, ('dp', 'seq'))
- grad_vectors: float32 [19, 1408], P(None, ('dp', 'seq'))
- grad_head_norms: float32 [8, 88], replicated
- grad_fc_bias: float32 [6144], replicated
The draws below stay inside these ranges and needn't reach their ends.
Inputs may be any that keep to these rules, and one draw needn't show every extreme that they name: `mt5_len`: every image has from 10 to 256 live mT5 tokens; some image has all 256.
All inputs are finite; a program needn't handle non-finite values.
Results may differ from the reference program's by a relative error of at most 0.018.
Values may be sent and summed in bfloat16 or wider, within the bound.
No kernel may reach another device: no remote copies, remote signals or barrier semaphores. Data moves between devices by JAX's collectives and lax.ppermute only.
A program may use at most 448 MiB of HBM per device.

```python
import jax
import jax.numpy as jnp
from jax import lax

D = 1408
HEADS = 16
FF = 6144
TD = 1024
CLIP = 77
MT5 = 256
MIN_MT5 = 10
GRID = 32
NV = 19
HD = 88
P_SIZE = 1024
TXT = 333
IMAGES = 16


def draw_vectors(key, part):
    noise = jax.random.normal(key, (NV, D), jnp.float32) * 0.3
    marks = jnp.zeros((NV, 1), jnp.float32).at[jnp.array([1, 3, 10, 16])].set(1.0)
    return (noise + marks).astype(jnp.bfloat16)


def draw_head_norms(key, part):
    noise = jax.random.normal(key, (8, HD), jnp.float32) * 0.3
    marks = jnp.zeros((8, 1), jnp.float32).at[jnp.array([0, 2, 4, 6])].set(1.0)
    return (noise + marks).astype(jnp.bfloat16)


def draw_mt5_len(key, part):
    length_key, slot_key = jax.random.split(key)
    lengths = jax.random.randint(length_key, (IMAGES,), MIN_MT5, MT5 + 1, dtype=jnp.int32)
    chosen = jax.random.randint(slot_key, (), 0, IMAGES, dtype=jnp.int32)
    return lengths.at[chosen].set(MT5)


def shard_levels(own_key, shape, pieces, low, high):
    level = 1.0
    for dim, shards_of in pieces:
        draws = jax.random.uniform(jax.random.fold_in(jax.random.fold_in(own_key, 6), dim), (shards_of,), jnp.float32, low / len(pieces), high / len(pieces))
        level = level * jnp.repeat(jnp.exp(draws), shape[dim] // shards_of).reshape((-1,) + (1,) * (len(shape) - 1 - dim))
    return level


def bell_draw(key, shape, width, most, cuts=(), held_as=jnp.bfloat16):
    factor_of = shard_levels(key, shape, cuts, -0.22, 0.18) if cuts else 1.0
    entries = jax.random.normal(key, shape, jnp.float32) * width * factor_of
    return jnp.minimum(jnp.maximum(entries, -most), most).astype(held_as)


def setup_inputs(seed: int = 0) -> dict:
    seeds = jax.random.split(jax.random.key(seed), 19)
    return {
        "hidden_in": bell_draw(seeds[0], (IMAGES, P_SIZE, D), 1.0, 6.0, ((0, 16), (1, 2))),
        "skip_in": bell_draw(seeds[1], (IMAGES, P_SIZE, D), 1.0, 6.0, ((0, 16), (1, 2))),
        "text": bell_draw(seeds[2], (IMAGES, TXT, TD), 1.0, 6.0, ((0, 16),)),
        "temb": bell_draw(seeds[3], (IMAGES, D), 1.0, 6.0, ((0, 16),), jnp.float32),
        "mt5_len": draw_mt5_len(jax.random.fold_in(seeds[18], 71), 0),
        "cotangent": bell_draw(seeds[5], (IMAGES, P_SIZE, D), 1.0, 6.0, ((0, 16), (1, 2))),
        "skip_w": bell_draw(seeds[6], (2 * D, D), (2 * D) ** -0.5, 0.109375, ((0, 32),)),
        "time_w": bell_draw(seeds[7], (D, D), D ** -0.5, 0.15625, ((0, 32),)),
        "qkv_w": bell_draw(seeds[8], (D, 3 * D), D ** -0.5, 0.15625, ((0, 32),)),
        "out_w": bell_draw(seeds[9], (D, D), (D // 16) ** -0.5, 0.625, ((0, 32),)),
        "q2_w": bell_draw(seeds[10], (D, D), D ** -0.5, 0.15625, ((0, 32),)),
        "kv2_w": bell_draw(seeds[11], (TD, 2 * D), TD ** -0.5, 0.1875, ((0, 32),)),
        "out2_w": bell_draw(seeds[12], (D, D), (D // 6) ** -0.5, 0.375, ((0, 32),)),
        "fc1_w": bell_draw(seeds[13], (D, FF), D ** -0.5, 0.15625, ((0, 32),)),
        "fc2_w": bell_draw(seeds[14], (FF, D), FF ** -0.5, 0.078125, ((1, 32),)),
        "vectors": draw_vectors(jax.random.fold_in(seeds[18], 71), 0),
        "head_norms": draw_head_norms(jax.random.fold_in(seeds[18], 71), 0),
        "fc_bias": bell_draw(seeds[17], (FF,), 0.5, 3.0),
    }


EPSILON = 1e-06
HIGHEST = lax.Precision.HIGHEST

@jax.custom_vjp
def low(v):
    return lax.optimization_barrier(v.astype(jnp.bfloat16)).astype(jnp.float32)

@jax.custom_vjp
def low_back(v):
    return v

def low_keep(v):
    return (low(v), None)

def low_pass(kept, grad):
    return (grad,)

def back_keep(v):
    return (v, None)

def back_low(kept, grad):
    return (low(grad),)
low.defvjp(low_keep, low_pass)
low_back.defvjp(back_keep, back_low)

def layer_norm(inputs, scales, offset):
    middle = lax.optimization_barrier(jnp.mean(inputs, axis=-1, keepdims=True))
    centred = inputs - middle
    variance = lax.optimization_barrier(jnp.mean(centred * centred, axis=-1, keepdims=True))
    return centred * lax.rsqrt(variance + EPSILON) * scales + offset

def head_norm(inputs, scales, offset):
    shaped = inputs.reshape(inputs.shape[:-1] + (HEADS, HD))
    return layer_norm(shaped, scales, offset).reshape(inputs.shape)

def rotate(inputs, cosine, sine_part):
    quarter = HD // 4
    shaped = inputs.reshape(inputs.shape[:-1] + (HEADS, 2, 2, quarter))
    first_half = shaped[..., 0, :]
    second = shaped[..., 1, :]
    cosine = cosine[:, None]
    sine_part = sine_part[:, None]
    turned = jnp.stack([first_half * cosine - second * sine_part, second * cosine + first_half * sine_part], axis=-2)
    return turned.reshape(inputs.shape)

def angles(index):
    quarter = HD // 4
    rows_pos = (index // GRID).astype(jnp.float32)
    cols_pos = (index % GRID).astype(jnp.float32)
    frequency = 10000.0 ** (-jnp.arange(quarter, dtype=jnp.float32) / quarter)
    coords = jnp.stack([rows_pos, cols_pos], axis=-1)
    phases = coords[:, :, None] * frequency
    return (jnp.cos(phases), jnp.sin(phases))

def matmul(left, right):
    return jnp.dot(left, right, precision=HIGHEST)

def attention(queries, keys, values, valid):
    query_heads = queries.reshape(queries.shape[0], HEADS, HD)
    key_heads = keys.reshape(keys.shape[0], HEADS, HD)
    value_heads = values.reshape(values.shape[0], HEADS, HD)
    raw_scores = low_back(jnp.einsum('qhd,khd->hqk', query_heads, key_heads, precision=HIGHEST))
    scores = jnp.where(valid[None, None, :], raw_scores * HD ** (-0.5), -1e+30)
    row_max = lax.optimization_barrier(jnp.max(scores, axis=-1, keepdims=True))
    exponent = jnp.exp(scores - row_max)
    probabilities = exponent / lax.optimization_barrier(jnp.sum(exponent, axis=-1, keepdims=True))
    output = jnp.einsum('hqk,khd->qhd', low(probabilities), value_heads, precision=HIGHEST)
    return low_back(low(output.reshape(queries.shape[0], D)))

def image_forward(weights, image_hidden, image_skip, image_text, image_temb, length):
    skip_w, time_w, qkv_w, out_w, q2_w, kv2_w, out2_w, fc1_w, fc2_w, rows, norms, inner_bias = weights
    joined = jnp.concatenate([image_hidden, image_skip], axis=-1)
    skip_proj = low_back(matmul(joined, skip_w) + rows[0])
    stream_zero = layer_norm(skip_proj, rows[1], rows[2])
    shift = low_back(matmul(low(jax.nn.silu(image_temb))[None], time_w)[0] + rows[5])
    attn_in = low(layer_norm(stream_zero, rows[3], rows[4]) + shift)
    qkv_out = low_back(matmul(attn_in, qkv_w) + jnp.concatenate([rows[6], rows[7], rows[8]]))
    cosine, sine_part = angles(jnp.arange(P_SIZE, dtype=jnp.int32))
    queries = low_back(low(rotate(head_norm(qkv_out[:, :D], norms[0], norms[1]), cosine, sine_part)))
    keys = low_back(low(rotate(head_norm(qkv_out[:, D:2 * D], norms[2], norms[3]), cosine, sine_part)))
    values = low_back(low(qkv_out[:, 2 * D:]))
    attended = attention(queries, keys, values, jnp.ones((P_SIZE,), dtype=bool))
    stream_one = stream_zero + low_back(matmul(attended, out_w) + rows[9])
    cross_in = low(layer_norm(stream_one, rows[10], rows[11]))
    query_two = low_back(matmul(cross_in, q2_w) + rows[12])
    query_norm = low_back(low(head_norm(query_two, norms[4], norms[5])))
    text_proj = low_back(matmul(image_text, kv2_w) + jnp.concatenate([rows[13], rows[14]]))
    key_norm = low_back(low(head_norm(text_proj[:, :D], norms[6], norms[7])))
    value_two = low_back(low(text_proj[:, D:]))
    valid = jnp.arange(TXT, dtype=jnp.int32) < CLIP + length
    cross_out = attention(query_norm, key_norm, value_two, valid)
    stream_two = stream_one + low_back(matmul(cross_out, out2_w) + rows[15])
    mlp_in = low(layer_norm(stream_two, rows[16], rows[17]))
    hidden_pre = low_back(matmul(mlp_in, fc1_w) + inner_bias)
    activated = low(jax.nn.gelu(hidden_pre, approximate=True))
    return stream_two + low_back(matmul(activated, fc2_w) + rows[18])

def reference(hidden_in, skip_in, text, temb, mt5_len, cotangent, skip_w, time_w, qkv_w, out_w, q2_w, kv2_w, out2_w, fc1_w, fc2_w, vectors, head_norms, fc_bias):
    weights = (skip_w.astype(jnp.float32), time_w.astype(jnp.float32), qkv_w.astype(jnp.float32), out_w.astype(jnp.float32), q2_w.astype(jnp.float32), kv2_w.astype(jnp.float32), out2_w.astype(jnp.float32), fc1_w.astype(jnp.float32), fc2_w.astype(jnp.float32), vectors.astype(jnp.float32), head_norms.astype(jnp.float32), fc_bias.astype(jnp.float32))

    def forward(params, all_hidden, all_skip, all_text, all_temb):

        def one_image(element):
            return image_forward(params, element[0], element[1], element[2], element[3], element[4])
        return lax.map(jax.checkpoint(one_image), (all_hidden, all_skip, all_text, all_temb, mt5_len))
    block_out, pull = jax.vjp(forward, weights, hidden_in.astype(jnp.float32), skip_in.astype(jnp.float32), text.astype(jnp.float32), temb)
    grad_weights, grad_hidden, grad_skip, grad_text, grad_temb = pull(cotangent.astype(jnp.float32))
    return (block_out, grad_hidden, grad_skip, grad_text, grad_temb, grad_weights[0], grad_weights[1], grad_weights[2], grad_weights[3], grad_weights[4], grad_weights[5], grad_weights[6], grad_weights[7], grad_weights[8], grad_weights[9], grad_weights[10], grad_weights[11])
```

```python
import math

import jax
import jax.numpy as jnp
from jax import lax
from jax.experimental import pallas as pl
from jax.experimental.pallas import tpu as pltpu
from jax.sharding import PartitionSpec as P

D = 1408
HEADS = 16
CLIP = 77
GRID = 32
HD = 88
TXT = 333
TXT_PAD = 384
LOCAL = HEADS // 2
HW = LOCAL * HD
AXES = ("dp", "seq")
SCALE = HD**-0.5
LOG2E = math.log2(math.e)

EPSILON = 1e-06

F32 = jnp.float32
BF16 = jnp.bfloat16


def layer_norm(inputs, scales, offset):
    middle = jnp.mean(inputs, axis=-1, keepdims=True)
    centred = inputs - middle
    variance = jnp.mean(centred * centred, axis=-1, keepdims=True)
    return centred * lax.rsqrt(variance + EPSILON) * scales + offset


def dot(left, right, left_dim=1, right_dim=0):
    return lax.dot_general(
        left, right, (((left_dim,), (right_dim,)), ((), ())), preferred_element_type=F32
    )


def column_sum(inputs, axis=0):
    return jnp.sum(inputs.astype(F32), axis=axis)


def core_swap(value):
    chips = lax.axis_size("dp")
    pairs = [(2 * i + s, 2 * i + 1 - s) for i in range(chips) for s in range(2)]
    return lax.ppermute(value, AXES, pairs)


def chip_swap(value, bit):
    chips = lax.axis_size("dp")
    pairs = [(2 * i + s, 2 * (i ^ (1 << bit)) + s) for i in range(chips) for s in range(2)]
    return lax.ppermute(value, AXES, pairs)


def chip_send(value, bit, from_own):
    chips = lax.axis_size("dp")
    pairs = [
        (2 * i + s, 2 * (i ^ (1 << bit)) + s)
        for i in range(chips)
        for s in range(2)
        if (((i >> bit) & 1) == s) == from_own
    ]
    return lax.ppermute(value, AXES, pairs)


def chip_bit(bit):
    return (lax.axis_index("dp") >> bit) & 1


def gather_blocks(block, order):
    have = []
    value = block
    for bit in order:
        other = chip_swap(value, bit)
        up = chip_bit(bit) == 1
        lower = jnp.where(up, other, value)
        upper = jnp.where(up, value, other)
        place = sum(1 for b in have if b > bit)
        value = jnp.stack([lower, upper], axis=place)
        have.append(bit)
    return value.reshape((-1,) + block.shape)


def scatter_blocks(value, order):
    bits = sorted(order, reverse=True)
    sources = [value.reshape((2,) * len(bits) + value.shape[1:])]
    for bit in order:
        place = bits.index(bit)
        mine = chip_bit(bit)

        def pick(source, index):
            return lax.dynamic_index_in_dim(source, index, axis=place, keepdims=False)

        leaving = sum(pick(s, 1 - mine).astype(F32) for s in sources).astype(BF16)
        arrived = chip_swap(leaving, bit)
        sources = [pick(s, mine) for s in sources] + [arrived]
        bits.remove(bit)
    return sum(s.astype(F32) for s in sources)


def bit_orders():
    count = lax.axis_size("dp").bit_length() - 1
    down = list(range(count - 1, -1, -1))
    third = count // 2
    first = down
    second = down[:-2] + [down[-1], down[-2]]
    last = down[third:][::-1][::-1] + down[:third]
    return first, second, last


def swap_groups(value):
    quarter = HD // 4
    return jnp.concatenate(
        [
            value[quarter : 2 * quarter],
            value[:quarter],
            value[3 * quarter :],
            value[2 * quarter : 3 * quarter],
        ],
        axis=0,
    )


def normalised(raw):
    middle = jnp.sum(raw, axis=0, keepdims=True) * (1.0 / HD)
    centred = raw - middle
    variance = jnp.sum(centred * centred, axis=0, keepdims=True) * (1.0 / HD)
    inverse = lax.rsqrt(variance + EPSILON)
    return centred * inverse, inverse


def apply_norm(raw, gain, offset, turn):
    unit, inverse = normalised(raw)
    value = unit * gain + offset
    if turn is not None:
        value = value * turn[0] + swap_groups(value) * turn[1]
    return value.astype(BF16), unit, inverse


def norm_back(grad, unit, inverse, gain, turn):
    if turn is not None:
        grad = grad * turn[0] + swap_groups(grad * turn[1])
    gain_terms = grad * unit
    inner = grad * gain
    mean_one = jnp.sum(inner, axis=0, keepdims=True) * (1.0 / HD)
    mean_two = jnp.sum(inner * unit, axis=0, keepdims=True) * (1.0 / HD)
    return inverse * (inner - mean_one - unit * mean_two), gain_terms, grad


def lane_fold(value):
    lanes = value.shape[1]
    return sum(value[:, i : i + 128] for i in range(0, lanes, 128))


def masked(scores, limit):
    if limit is None:
        return scores
    index = lax.broadcasted_iota(jnp.int32, scores.shape, 0)
    return jnp.where(index < limit, scores, -1e30)


def attention_forward(rope, step):
    def body(*refs):
        if rope:
            q_ref, k_ref, v_ref, norm_ref, cos_ref, sin_ref, out_ref, log_ref = refs
            turn = (cos_ref[...], sin_ref[...])
            limit = None
        else:
            limit_ref, q_ref, k_ref, v_ref, norm_ref, out_ref, log_ref = refs
            turn = None
            limit = limit_ref[0] + CLIP
        norms = norm_ref[...]
        queries = apply_norm(q_ref[0], norms[:, 0:1], norms[:, 1:2], turn)[0]
        keys = apply_norm(k_ref[0], norms[:, 2:3], norms[:, 3:4], turn)[0]
        values = v_ref[0].astype(BF16)
        for start in range(0, queries.shape[1], step):
            part = queries[:, start : start + step]
            scores = masked(dot(keys, part, 0, 0) * (SCALE * LOG2E), limit)
            top = jnp.max(scores, axis=0, keepdims=True)
            weights = jnp.exp2(scores - top)
            total = jnp.sum(weights, axis=0, keepdims=True)
            output = dot(values, weights.astype(BF16))
            out_ref[0, :, start : start + step] = (output / total).astype(BF16)
            log_ref[0, :, start : start + step] = top + jnp.log2(total)

    return body


def attention_backward(rope, step):
    def body(*refs):
        if rope:
            q_ref, k_ref, v_ref, grad_ref, log_ref, norm_ref, cos_ref, sin_ref = refs[:8]
            dq_ref, dk_ref, dv_ref, sums_ref = refs[8:]
            turn = (cos_ref[...], sin_ref[...])
            limit = None
        else:
            limit_ref, q_ref, k_ref, v_ref, grad_ref, log_ref, norm_ref = refs[:7]
            dq_ref, dk_ref, dv_ref, sums_ref = refs[7:]
            turn = None
            limit = limit_ref[0] + CLIP
        norms = norm_ref[...]
        queries, q_unit, q_inverse = apply_norm(q_ref[0], norms[:, 0:1], norms[:, 1:2], turn)
        keys, k_unit, k_inverse = apply_norm(k_ref[0], norms[:, 2:3], norms[:, 3:4], turn)
        values = v_ref[0].astype(BF16)
        grads = grad_ref[0]
        logs = log_ref[0]
        query_parts = []
        key_sum = jnp.zeros(keys.shape, F32)
        value_sum = jnp.zeros(keys.shape, F32)
        for start in range(0, queries.shape[1], step):
            part = queries[:, start : start + step]
            grad_part = grads[:, start : start + step]
            scores = masked(dot(keys, part, 0, 0) * (SCALE * LOG2E), limit)
            weights = jnp.exp2(scores - logs[:, start : start + step])
            grad_weights = dot(values, grad_part, 0, 0)
            inner = jnp.sum(weights * grad_weights, axis=0, keepdims=True)
            grad_scores = (weights * (grad_weights - inner)).astype(BF16)
            query_parts.append(dot(keys, grad_scores))
            key_sum = key_sum + dot(part, grad_scores, 1, 1)
            value_sum = value_sum + dot(grad_part, weights.astype(BF16), 1, 1)
        grad_q = (jnp.concatenate(query_parts, axis=1) * SCALE).astype(BF16).astype(F32)
        grad_k = (key_sum * SCALE).astype(BF16).astype(F32)
        raw_q, q_gain, q_offset = norm_back(grad_q, q_unit, q_inverse, norms[:, 0:1], turn)
        raw_k, k_gain, k_offset = norm_back(grad_k, k_unit, k_inverse, norms[:, 2:3], turn)
        dq_ref[0] = raw_q.astype(BF16)
        dk_ref[0] = raw_k.astype(BF16)
        dv_ref[0] = value_sum.astype(BF16)

        @pl.when(pl.program_id(0) == 0)
        def _():
            sums_ref[...] = jnp.zeros(sums_ref.shape, F32)

        for place, terms in enumerate((q_gain, q_offset, k_gain, k_offset)):
            sums_ref[place] += lane_fold(terms)

    return body


def head_spec(width, shift=0):
    return pl.BlockSpec((1, HD, width), lambda h, *_: (h + shift, 0, 0))


def whole_spec(shape):
    return pl.BlockSpec(shape, lambda h, *_: (0,) * len(shape))


def self_attention(raw, norms, cosine, sine):
    tokens = raw.shape[2]
    return pl.pallas_call(
        attention_forward(True, 256),
        grid=(LOCAL,),
        in_specs=[head_spec(tokens, s) for s in (0, LOCAL, 2 * LOCAL)]
        + [whole_spec((HD, 4)), whole_spec((HD, tokens)), whole_spec((HD, tokens))],
        out_specs=[head_spec(tokens), pl.BlockSpec((1, 1, tokens), lambda h: (h, 0, 0))],
        out_shape=[
            jax.ShapeDtypeStruct((LOCAL, HD, tokens), BF16),
            jax.ShapeDtypeStruct((LOCAL, 1, tokens), F32),
        ],
        name="self_forward",
    )(raw, raw, raw, norms, cosine, sine)


def self_attention_back(raw, grads, logs, norms, cosine, sine):
    tokens = raw.shape[2]
    return pl.pallas_call(
        attention_backward(True, 256),
        grid=(LOCAL,),
        in_specs=[head_spec(tokens, s) for s in (0, LOCAL, 2 * LOCAL)]
        + [head_spec(tokens), pl.BlockSpec((1, 1, tokens), lambda h: (h, 0, 0))]
        + [whole_spec((HD, 4)), whole_spec((HD, tokens)), whole_spec((HD, tokens))],
        out_specs=[head_spec(tokens)] * 3 + [whole_spec((4, HD, 128))],
        out_shape=[jax.ShapeDtypeStruct((LOCAL, HD, tokens), BF16)] * 3
        + [jax.ShapeDtypeStruct((4, HD, 128), F32)],
        name="self_backward",
    )(raw, raw, raw, grads, logs, norms, cosine, sine)


def cross_attention(limit, raw_q, raw_text, norms):
    tokens = raw_q.shape[2]
    slots = raw_text.shape[2]
    return pl.pallas_call(
        attention_forward(False, 512),
        grid_spec=pltpu.PrefetchScalarGridSpec(
            num_scalar_prefetch=1,
            grid=(LOCAL,),
            in_specs=[head_spec(tokens), head_spec(slots), head_spec(slots, LOCAL)]
            + [whole_spec((HD, 4))],
            out_specs=[
                head_spec(tokens),
                pl.BlockSpec((1, 1, tokens), lambda h, *_: (h, 0, 0)),
            ],
        ),
        out_shape=[
            jax.ShapeDtypeStruct((LOCAL, HD, tokens), BF16),
            jax.ShapeDtypeStruct((LOCAL, 1, tokens), F32),
        ],
        name="cross_forward",
    )(limit, raw_q, raw_text, raw_text, norms)


def cross_attention_back(limit, raw_q, raw_text, grads, logs, norms):
    tokens = raw_q.shape[2]
    slots = raw_text.shape[2]
    return pl.pallas_call(
        attention_backward(False, 512),
        grid_spec=pltpu.PrefetchScalarGridSpec(
            num_scalar_prefetch=1,
            grid=(LOCAL,),
            in_specs=[head_spec(tokens), head_spec(slots), head_spec(slots, LOCAL)]
            + [head_spec(tokens), pl.BlockSpec((1, 1, tokens), lambda h, *_: (h, 0, 0))]
            + [whole_spec((HD, 4))],
            out_specs=[head_spec(tokens), head_spec(slots), head_spec(slots)]
            + [whole_spec((4, HD, 128))],
        ),
        out_shape=[
            jax.ShapeDtypeStruct((LOCAL, HD, tokens), BF16),
            jax.ShapeDtypeStruct((LOCAL, HD, slots), BF16),
            jax.ShapeDtypeStruct((LOCAL, HD, slots), BF16),
            jax.ShapeDtypeStruct((4, HD, 128), F32),
        ],
        name="cross_backward",
    )(limit, raw_q, raw_text, raw_text, grads, logs, norms)


def rotary_tables(positions):
    quarter = HD // 4
    frequency = 10000.0 ** (-jnp.arange(quarter, dtype=F32) / quarter)
    rows = (positions // GRID).astype(F32)
    columns = (positions % GRID).astype(F32)
    row_phase = frequency[:, None] * rows[None, :]
    column_phase = frequency[:, None] * columns[None, :]
    phases = jnp.concatenate([row_phase, row_phase, column_phase, column_phase], axis=0)
    signs = jnp.where((jnp.arange(HD) // quarter) % 2 == 0, -1.0, 1.0).astype(F32)
    return jnp.cos(phases), jnp.sin(phases) * signs[:, None]


def shards(
    hidden_in,
    skip_in,
    text,
    temb,
    mt5_len,
    cotangent,
    skip_w,
    time_w,
    qkv_w,
    out_w,
    q2_w,
    kv2_w,
    out2_w,
    fc1_w,
    fc2_w,
    vectors,
    head_norms,
    fc_bias,
):
    chips = lax.axis_size("dp")
    core = lax.axis_index("seq")
    chip = lax.axis_index("dp")
    first_core = core == 0
    half_tokens = hidden_in.shape[1]
    hidden_units = fc_bias.shape[0]
    half_units = hidden_units // 2
    top_bit = chips.bit_length() - 2
    order_a, order_b, order_c = bit_orders()
    low_a = [b for b in order_a if b != top_bit]
    low_c = [b for b in order_c if b != top_bit]
    own_half = (chip >> top_bit) == core

    def ordered(mine, other, axis):
        return jnp.where(
            first_core,
            jnp.concatenate([mine, other], axis=axis),
            jnp.concatenate([other, mine], axis=axis),
        )

    def take(value, index, axis):
        return lax.dynamic_index_in_dim(value, index, axis=axis, keepdims=False)

    def both(value):
        return jnp.concatenate([value, core_swap(value)], axis=0)

    def fold(partial):
        return partial[:half_tokens] + core_swap(partial[half_tokens:])

    def column_block(weight, groups):
        rows_here = weight.shape[0]
        halves = weight.reshape(rows_here, groups, 2, -1)
        mine = take(halves, core, 2)
        other = core_swap(take(halves, 1 - core, 2))
        return ordered(mine, other, 0).reshape(2 * rows_here, -1)

    def row_block(weight):
        return ordered(weight, core_swap(weight), 0)

    def half_of(vector):
        return take(vector.reshape(vector.shape[:-1] + (2, -1)), core, vector.ndim - 1)

    def spread(half):
        zeros = jnp.zeros_like(half)
        return ordered(half, zeros, half.ndim - 1)

    def gather_rows(block, order):
        moved = chip_send(block, top_bit, True)
        return gather_blocks(jnp.where(own_half, block, moved), order)

    def scatter_rows(value, order):
        partial = scatter_blocks(value, order)
        return partial + chip_send(partial.astype(BF16), top_bit, False).astype(F32)

    silu_low = jax.nn.silu(temb).astype(BF16)
    vector_pair = ordered(vectors[None], core_swap(vectors)[None], 0)
    small = jnp.concatenate([vector_pair.reshape(-1), silu_low.reshape(-1)])
    small_all = gather_blocks(small, order_a)
    count = vector_pair.size
    vector_full = (
        small_all[:, :count]
        .reshape(chips, 2, vectors.shape[0], -1)
        .transpose(2, 0, 1, 3)
        .reshape(vectors.shape[0], D)
    )
    silu_all = small_all[:, count:]

    skip_rows = 2 * skip_w.shape[0]
    time_rows = 2 * time_w.shape[0]
    item_one = gather_rows(
        jnp.concatenate([row_block(skip_w), row_block(time_w)], axis=0), low_a
    )
    skip_mine = item_one[:, :skip_rows].reshape(D, D)
    time_mine = item_one[:, skip_rows:].reshape(HW, D)
    qkv_mine = gather_blocks(column_block(qkv_w, 3), order_b).reshape(D, 3 * HW)
    out_pair = gather_rows(jnp.stack([row_block(out_w), row_block(out2_w)]), low_c)
    out_mine = out_pair[:, 0].reshape(HW, D)
    out2_mine = out_pair[:, 1].reshape(HW, D)
    q2_rows = 2 * q2_w.shape[0]
    kv_rows = 2 * kv2_w.shape[0]
    kv_block = column_block(kv2_w, 2)
    item_four = gather_blocks(
        jnp.concatenate(
            [column_block(q2_w, 1), kv_block[:, :HW], kv_block[:, HW:]], axis=0
        ),
        order_c,
    )
    q2_mine = item_four[:, :q2_rows].reshape(D, HW)
    k2_mine = item_four[:, q2_rows : q2_rows + kv_rows].reshape(-1, HW)
    v2_mine = item_four[:, q2_rows + kv_rows :].reshape(-1, HW)
    fc1_mine = gather_blocks(column_block(fc1_w, 1), order_a).reshape(D, half_units)
    fc2_mine = gather_blocks(column_block(fc2_w.T, 1), order_b).reshape(D, half_units)

    rows = vector_full.astype(F32)
    norms = head_norms.astype(F32)
    norm_columns = norms.T
    hidden = hidden_in[0]
    skipped = skip_in[0]
    own_input = jnp.where(first_core, hidden, skipped)
    joined = jnp.concatenate(
        [own_input, core_swap(jnp.where(first_core, skipped, hidden))], axis=0
    )
    grads_all = both(cotangent[0])
    text_low = jnp.pad(text[0], ((0, TXT_PAD - TXT), (0, 0)))
    limit = mt5_len.astype(jnp.int32)
    token = jnp.arange(half_tokens, dtype=jnp.int32)
    positions = jnp.concatenate([core * half_tokens + token, (1 - core) * half_tokens + token])
    cosine, sine = rotary_tables(positions)

    skip_proj = fold(dot(joined, skip_mine)) + rows[0]
    stream_zero = layer_norm(skip_proj, rows[1], rows[2])
    shift_part = dot(half_of(silu_low), time_mine)
    shift = shift_part + core_swap(shift_part) + rows[5]
    attn_in = (layer_norm(stream_zero, rows[3], rows[4]) + shift).astype(BF16)
    attn_all = both(attn_in)
    raw = dot(qkv_mine, attn_all, 0, 1) + half_of(rows[6:9]).reshape(-1)[:, None]
    raw = raw.reshape(3 * LOCAL, HD, -1)
    attended, logs = self_attention(raw, norm_columns[:, :4], cosine, sine)
    attended = attended.reshape(HW, -1)
    stream_one = stream_zero + (fold(dot(attended, out_mine, 0, 0)) + rows[9])
    cross_in = layer_norm(stream_one, rows[10], rows[11]).astype(BF16)
    cross_all = both(cross_in)
    raw_two = (dot(q2_mine, cross_all, 0, 1) + half_of(rows[12])[:, None]).reshape(LOCAL, HD, -1)
    text_raw = jnp.concatenate(
        [
            dot(k2_mine, text_low, 0, 1) + half_of(rows[13])[:, None],
            dot(v2_mine, text_low, 0, 1) + half_of(rows[14])[:, None],
        ],
        axis=0,
    ).reshape(2 * LOCAL, HD, TXT_PAD)
    crossed, cross_logs = cross_attention(limit, raw_two, text_raw, norm_columns[:, 4:])
    crossed = crossed.reshape(HW, -1)
    stream_two = stream_one + (fold(dot(crossed, out2_mine, 0, 0)) + rows[15])
    mlp_in = layer_norm(stream_two, rows[16], rows[17]).astype(BF16)
    mlp_all = both(mlp_in)
    hidden_pre = dot(mlp_all, fc1_mine) + half_of(fc_bias.astype(F32))

    def gelu_tanh(inner):
        return jax.nn.gelu(inner, approximate=True)

    activated = gelu_tanh(hidden_pre).astype(BF16)
    block_out = stream_two + (fold(dot(activated, fc2_mine, 1, 1)) + rows[18])

    bias_fc2 = column_sum(cotangent[0])
    grad_pre = jax.vjp(gelu_tanh, hidden_pre)[1](dot(grads_all, fc2_mine))[0].astype(BF16)
    fc2_terms = dot(grads_all, activated, 0, 0).astype(BF16).reshape(chips, -1, half_units)
    fc1_terms = dot(mlp_all, grad_pre, 0, 0).astype(BF16).reshape(chips, -1, half_units)
    grad_inner_bias = spread(column_sum(grad_pre))
    grad_mlp_in = fold(dot(grad_pre, fc1_mine, 1, 1))
    norm_pull = jax.vjp(layer_norm, stream_two, rows[16], rows[17])[1]
    from_mlp, gain_two, offset_two = norm_pull(grad_mlp_in)
    grad_two = cotangent[0].astype(F32) + from_mlp

    cross_grad = grad_two.astype(BF16)
    bias_out2 = column_sum(cross_grad)
    cross_grad_all = both(cross_grad)
    out2_terms = dot(crossed, cross_grad_all).astype(BF16)
    grad_crossed = dot(out2_mine, cross_grad_all, 1, 1).astype(BF16).reshape(LOCAL, HD, -1)
    dq2, dk2, dv2, cross_sums = cross_attention_back(
        limit, raw_two, text_raw, grad_crossed, cross_logs, norm_columns[:, 4:]
    )
    dq2 = dq2.reshape(HW, -1)
    dk2 = dk2.reshape(HW, -1)
    dv2 = dv2.reshape(HW, -1)
    q2_terms = dot(cross_all, dq2, 0, 1).astype(BF16)
    k2_terms = dot(text_low, dk2, 0, 1).astype(BF16)
    v2_terms = dot(text_low, dv2, 0, 1).astype(BF16)
    text_part = dot(dk2, k2_mine, 0, 1) + dot(dv2, v2_mine, 0, 1)
    grad_text = (text_part + core_swap(text_part))[:TXT]
    grad_cross_in = fold(dot(dq2, q2_mine, 0, 1))
    third_pull = jax.vjp(layer_norm, stream_one, rows[10], rows[11])[1]
    from_cross, gain_three, offset_three = third_pull(grad_cross_in)
    grad_one = grad_two + from_cross

    attn_grad = grad_one.astype(BF16)
    bias_out = column_sum(attn_grad)
    attn_grad_all = both(attn_grad)
    out_terms = dot(attended, attn_grad_all).astype(BF16)
    grad_attended = dot(out_mine, attn_grad_all, 1, 1).astype(BF16).reshape(LOCAL, HD, -1)
    dq, dk, dv, self_sums = self_attention_back(
        raw, grad_attended, logs, norm_columns[:, :4], cosine, sine
    )
    qkv_grad = jnp.concatenate([dq, dk, dv], axis=0).reshape(3 * HW, -1)
    qkv_terms = dot(attn_all, qkv_grad, 0, 1).astype(BF16).reshape(chips, -1, 3 * HW)
    grad_attn_in = fold(dot(qkv_grad, qkv_mine, 0, 1))
    first_pull = jax.vjp(layer_norm, stream_zero, rows[3], rows[4])[1]
    from_attn, gain_one, offset_one = first_pull(grad_attn_in)
    grad_zero = grad_one + from_attn
    shift_sum = jnp.sum(grad_attn_in, axis=0, keepdims=True)
    shift_low = (shift_sum + core_swap(shift_sum)).astype(BF16)
    silu_part = dot(shift_low, time_mine, 1, 1)
    silu_grad = ordered(silu_part, core_swap(silu_part), 1)
    grad_temb = jax.vjp(jax.nn.silu, temb)[1](silu_grad)[0]
    shift_all = gather_blocks(shift_low.reshape(-1), order_a)
    device = 2 * chip + core
    time_here = time_w.shape[0]
    silu_here = lax.dynamic_slice_in_dim(silu_all, device * time_here, time_here, axis=1)
    grad_time = dot(silu_here, shift_all, 0, 0)

    skip_pull = jax.vjp(layer_norm, skip_proj, rows[1], rows[2])[1]
    grad_proj, gain_skip, offset_skip = skip_pull(grad_zero)
    proj_low = grad_proj.astype(BF16)
    bias_skip = column_sum(proj_low)
    proj_all = both(proj_low)
    skip_terms = dot(joined, proj_all, 0, 0).astype(BF16)
    grad_input = dot(proj_all, skip_mine, 1, 1)
    other_input = core_swap(grad_input[half_tokens:])
    grad_hidden = jnp.where(first_core, grad_input[:half_tokens], other_input)
    grad_skip = jnp.where(first_core, other_input, grad_input[:half_tokens])

    def column_result(value, groups):
        own_rows = value.shape[0] // 2
        parts = value.reshape(2, own_rows, groups, -1)
        mine = take(parts, core, 0)
        other = core_swap(take(parts, 1 - core, 0))
        return ordered(mine[:, :, None], other[:, :, None], 2).reshape(own_rows, -1)

    def row_result(value):
        own_rows = value.shape[0] // 2
        parts = value.reshape(2, own_rows, D)
        other = core_swap(take(parts, 1 - core, 0))
        return jnp.where(own_half, take(parts, core, 0), other)

    back = lambda order: order[::-1]
    grad_fc2 = column_result(scatter_blocks(fc2_terms, back(order_b)), 1).T
    grad_fc1 = column_result(scatter_blocks(fc1_terms, back(order_a)), 1)
    item_four_terms = jnp.concatenate(
        [
            q2_terms.reshape(chips, q2_rows, HW),
            k2_terms.reshape(chips, kv_rows, HW),
            v2_terms.reshape(chips, kv_rows, HW),
        ],
        axis=1,
    )
    item_four_grad = scatter_blocks(item_four_terms, back(order_c))
    grad_q2 = column_result(item_four_grad[:q2_rows], 1)
    grad_kv2 = column_result(
        jnp.concatenate(
            [item_four_grad[q2_rows : q2_rows + kv_rows], item_four_grad[q2_rows + kv_rows :]],
            axis=1,
        ),
        2,
    )
    half_chips = chips // 2
    pair_terms = jnp.stack(
        [out_terms.reshape(half_chips, -1, D), out2_terms.reshape(half_chips, -1, D)], axis=1
    )
    pair_grad = scatter_rows(pair_terms, back(low_c))
    grad_out = row_result(pair_grad[0])
    grad_out2 = row_result(pair_grad[1])
    grad_qkv = column_result(scatter_blocks(qkv_terms, back(order_b)), 3)
    skip_grad = scatter_rows(skip_terms.reshape(half_chips, -1, D), back(low_a))
    grad_skipw = row_result(skip_grad)

    def bias_of(grads):
        return spread(column_sum(grads, axis=1).reshape(-1, HW))

    bias_qkv = bias_of(qkv_grad)
    owner = first_core.astype(F32)
    vector_grad = jnp.stack(
        [
            bias_skip,
            gain_skip,
            offset_skip,
            gain_one,
            offset_one,
            shift_low[0].astype(F32) * owner,
            bias_qkv[0],
            bias_qkv[1],
            bias_qkv[2],
            bias_out,
            gain_three,
            offset_three,
            bias_of(dq2)[0],
            bias_of(dk2)[0],
            bias_of(dv2)[0],
            bias_out2,
            gain_two,
            offset_two,
            bias_fc2,
        ]
    )
    norm_grad = jnp.concatenate([jnp.sum(self_sums, axis=2), jnp.sum(cross_sums, axis=2)])
    packed = jnp.concatenate(
        [vector_grad.reshape(-1), norm_grad.reshape(-1), grad_inner_bias.reshape(-1)]
    )
    packed = packed + core_swap(packed)
    for bit in order_a:
        packed = packed + chip_swap(packed, bit)
    vector_count = vector_grad.size
    norm_count = norm_grad.size
    vector_here = vectors.shape[1]
    grad_vectors = lax.dynamic_slice_in_dim(
        packed[:vector_count].reshape(vector_grad.shape), device * vector_here, vector_here, axis=1
    )
    norm_total = packed[vector_count : vector_count + norm_count].reshape(norm_grad.shape)
    bias_total = packed[vector_count + norm_count :]
    return (
        block_out[None],
        grad_hidden[None],
        grad_skip[None],
        grad_text[None],
        grad_temb,
        grad_skipw,
        grad_time,
        grad_qkv,
        grad_out,
        grad_q2,
        grad_kv2,
        grad_out2,
        grad_fc1,
        grad_fc2,
        grad_vectors,
        norm_total,
        bias_total,
    )


def solution(mesh):
    tokens = P("dp", "seq", None)
    rows = P(AXES, None)
    columns = P(None, AXES)
    return jax.shard_map(
        shards,
        mesh=mesh,
        in_specs=(
            tokens,
            tokens,
            P("dp", None, None),
            P("dp", None),
            P("dp"),
            tokens,
            rows,
            rows,
            rows,
            rows,
            rows,
            rows,
            rows,
            rows,
            columns,
            columns,
            P(),
            P(),
        ),
        out_specs=(
            tokens,
            tokens,
            tokens,
            P("dp", None, None),
            P("dp", None),
            rows,
            rows,
            rows,
            rows,
            rows,
            rows,
            rows,
            rows,
            columns,
            columns,
            P(),
            P(),
        ),
        check_vma=False,
    )
```

```python
import math

import jax
import jax.numpy as jnp
from jax import lax
from jax.experimental import pallas as pl
from jax.experimental.pallas import tpu as pltpu
from jax.sharding import PartitionSpec as P

D = 1408
HEADS = 16
CLIP = 77
GRID = 32
HD = 88
TXT = 333
TXT_PAD = 384
LOCAL = HEADS // 2
HW = LOCAL * HD
AXES = ("dp", "seq")
SCALE = HD**-0.5
LOG2E = math.log2(math.e)

EPSILON = 1e-06

F32 = jnp.float32
BF16 = jnp.bfloat16


def layer_norm(inputs, scales, offset):
    middle = jnp.mean(inputs, axis=-1, keepdims=True)
    centred = inputs - middle
    variance = jnp.mean(centred * centred, axis=-1, keepdims=True)
    return centred * lax.rsqrt(variance + EPSILON) * scales + offset


def dot(left, right, left_dim=1, right_dim=0):
    return lax.dot_general(
        left, right, (((left_dim,), (right_dim,)), ((), ())), preferred_element_type=F32
    )


def column_sum(inputs, axis=0):
    return jnp.sum(inputs.astype(F32), axis=axis)


def core_swap(value):
    chips = lax.axis_size("dp")
    pairs = [(2 * i + s, 2 * i + 1 - s) for i in range(chips) for s in range(2)]
    return lax.ppermute(value, AXES, pairs)


def masks_of(chips):
    if chips == 16:
        return (1, 2, 4, 12)
    if chips == 64:
        return (1, 3, 4, 12, 16, 48)
    return tuple(1 << b for b in range(chips.bit_length() - 1))


def exchange_orders(chips):
    moves = masks_of(chips)
    half = len(moves) // 2
    first, second = moves[:half], moves[half:]
    return (
        (first + second, second + first),
        (first[::-1] + second[::-1], second[::-1] + first[::-1]),
    )


def exchange_rows(chips):
    moves = masks_of(chips)[:-1]
    return (
        (moves, moves[-1:] + moves[:-1]),
        (moves[1:] + moves[:1], moves[1:-1] + moves[-1:] + moves[:1]),
    )


def chip_swap(value, moves):
    chips = lax.axis_size("dp")
    pairs = [(2 * i + s, 2 * (i ^ moves[s]) + s) for i in range(chips) for s in range(2)]
    return lax.ppermute(value, AXES, pairs)


def chip_send(value, from_own):
    chips = lax.axis_size("dp")
    move = masks_of(chips)[-1]
    pairs = [
        (2 * i + s, 2 * (i ^ move) + s)
        for i in range(chips)
        for s in range(2)
        if ((2 * i // chips) == s) == from_own
    ]
    return lax.ppermute(value, AXES, pairs)


def tie(value, milestone):
    return value if milestone is None else lax.optimization_barrier((value, milestone))[0]


def chip_of_place(order, base):
    count = len(order[0])
    place = jnp.arange(1 << count, dtype=jnp.int32)
    chip = [base + jnp.zeros_like(place) for _ in range(2)]
    for step in range(count):
        bit = (place >> (count - 1 - step)) & 1
        chip = [c ^ (bit * o[step]) for c, o in zip(chip, order)]
    return jnp.where(lax.axis_index("seq") == 0, chip[0], chip[1])


def place_of_chip(order, target, base):
    count = len(order[0])
    both_cores = []
    for moves in order:
        columns = {}
        for code in range(1 << count):
            mask = 0
            for step in range(count):
                if (code >> (count - 1 - step)) & 1:
                    mask ^= moves[step]
            columns[mask] = code
        difference = target ^ base
        place = jnp.zeros_like(difference)
        for bit in range(max(columns).bit_length()):
            place = place ^ (((difference >> bit) & 1) * columns[1 << bit])
        both_cores.append(place)
    return jnp.where(lax.axis_index("seq") == 0, both_cores[0], both_cores[1])


def gather_group(items, after=None):
    values = [block[None] for block, _, _ in items]
    steps = [len(order[0]) + (own is not None) for _, order, own in items]
    others = [None] * len(items)
    if after is not None:
        values = list(lax.optimization_barrier((tuple(values), after))[0])
    for step in range(max(steps)):
        for i, (_, order, own) in enumerate(items):
            if own is not None and step == 0:
                others[i] = chip_send(values[i], True)
            else:
                move = steps[i] - 1 - step
                others[i] = chip_swap(values[i], (order[0][move], order[1][move]))
        values, others = (
            list(part) for part in lax.optimization_barrier((tuple(values), tuple(others)))
        )
        if step == max(steps) - 1:
            break
        for i, (_, _, own) in enumerate(items):
            if own is not None and step == 0:
                values[i] = jnp.where(own, values[i], others[i])
            else:
                values[i] = jnp.concatenate([values[i], others[i]], axis=0)
    return list(zip(values, others))


def scatter_group(items, ties=()):
    sources = [[kept] for kept, _, _, _ in items]
    leaving = [leave for _, leave, _, _ in items]
    count = max(len(order[0]) + rows for _, _, order, rows in items)
    for step in range(count):
        arrived = []
        for i, (_, _, order, rows) in enumerate(items):
            if rows and step == len(order[0]):
                arrived.append(chip_send(leaving[i], False))
            else:
                arrived.append(chip_swap(leaving[i], (order[0][step], order[1][step])))
        milestone = ties[step] if step < len(ties) else ()
        arrived = lax.optimization_barrier((tuple(arrived), milestone))[0]
        for i, (_, _, order, rows) in enumerate(items):
            sources[i].append(arrived[i])
            if step + 1 < len(order[0]):
                half = sources[i][0].shape[0] // 2
                leaving[i] = sum(s[half:].astype(F32) for s in sources[i]).astype(BF16)
                sources[i] = [s[:half] for s in sources[i]]
            elif step + 1 < count:
                total = sum(s.astype(F32) for s in sources[i])
                leaving[i] = total.astype(BF16)
                sources[i] = [total]
    return [sum(s.astype(F32) for s in terms)[0] for terms in sources]


def assemble(lower, upper, index):
    half = lower.shape[0]
    count = index.shape[0]

    def body(index_ref, lower_ref, upper_ref, out_ref, sems):
        for j in range(count):
            source = index_ref[j]

            @pl.when(source < half)
            def _():
                pltpu.make_async_copy(lower_ref.at[source], out_ref.at[j], sems.at[j]).start()

            @pl.when(source >= half)
            def _():
                pltpu.make_async_copy(
                    upper_ref.at[source - half], out_ref.at[j], sems.at[j]
                ).start()

        for j in range(count):
            pltpu.make_async_copy(lower_ref.at[0], out_ref.at[j], sems.at[j]).wait()

    shape = (count,) + lower.shape[1:]
    return pl.pallas_call(
        body,
        grid_spec=pltpu.PrefetchScalarGridSpec(
            num_scalar_prefetch=1,
            grid=(1,),
            in_specs=[pl.BlockSpec(memory_space=pl.ANY)] * 2,
            out_specs=pl.BlockSpec(shape, lambda i, *_: (0, 0, 0)),
            scratch_shapes=[pltpu.SemaphoreType.DMA((count,))],
        ),
        out_shape=jax.ShapeDtypeStruct(shape, lower.dtype),
        name="assemble",
    )(index, lower, upper)


def reorder(value, index):
    count = index.shape[0]
    half = count // 2
    shape = (half,) + value.shape[1:]

    def body(index_ref, value_ref, lower_ref, upper_ref, sems):
        places = [lower_ref.at[j] for j in range(half)] + [upper_ref.at[j] for j in range(half)]
        for j, place in enumerate(places):
            pltpu.make_async_copy(value_ref.at[index_ref[j]], place, sems.at[j]).start()
        for j, place in enumerate(places):
            pltpu.make_async_copy(value_ref.at[0], place, sems.at[j]).wait()

    return pl.pallas_call(
        body,
        grid_spec=pltpu.PrefetchScalarGridSpec(
            num_scalar_prefetch=1,
            grid=(1,),
            in_specs=[pl.BlockSpec(memory_space=pl.ANY)],
            out_specs=[pl.BlockSpec(shape, lambda i, *_: (0, 0, 0))] * 2,
            scratch_shapes=[pltpu.SemaphoreType.DMA((count,))],
        ),
        out_shape=[jax.ShapeDtypeStruct(shape, value.dtype)] * 2,
        name="reorder",
    )(index, value)


def swap_groups(value):
    quarter = HD // 4
    return jnp.concatenate(
        [
            value[quarter : 2 * quarter],
            value[:quarter],
            value[3 * quarter :],
            value[2 * quarter : 3 * quarter],
        ],
        axis=0,
    )


def normalised(raw):
    middle = jnp.sum(raw, axis=0, keepdims=True) * (1.0 / HD)
    centred = raw - middle
    variance = jnp.sum(centred * centred, axis=0, keepdims=True) * (1.0 / HD)
    inverse = lax.rsqrt(variance + EPSILON)
    return centred * inverse, inverse


def apply_norm(raw, gain, offset, turn):
    unit, inverse = normalised(raw)
    value = unit * gain + offset
    if turn is not None:
        value = value * turn[0] + swap_groups(value) * turn[1]
    return value.astype(BF16), unit, inverse


def norm_back(grad, unit, inverse, gain, turn):
    if turn is not None:
        grad = grad * turn[0] + swap_groups(grad * turn[1])
    gain_terms = grad * unit
    inner = grad * gain
    mean_one = jnp.sum(inner, axis=0, keepdims=True) * (1.0 / HD)
    mean_two = jnp.sum(inner * unit, axis=0, keepdims=True) * (1.0 / HD)
    return inverse * (inner - mean_one - unit * mean_two), gain_terms, grad


def lane_fold(value):
    lanes = value.shape[1]
    return sum(value[:, i : i + 128] for i in range(0, lanes, 128))


def masked(scores, limit):
    if limit is None:
        return scores
    index = lax.broadcasted_iota(jnp.int32, scores.shape, 0)
    return jnp.where(index < limit, scores, -1e30)


def attention_forward(rope, step):
    def body(*refs):
        if rope:
            raw_ref, norm_ref, cos_ref, sin_ref, out_ref, log_ref = refs
            q_ref, k_ref, v_ref = (raw_ref.at[i] for i in range(3))
            turn = (cos_ref[...], sin_ref[...])
            limit = None
        else:
            limit_ref, q_ref, k_ref, v_ref, norm_ref, out_ref, log_ref = refs
            turn = None
            limit = limit_ref[0] + CLIP
        norms = norm_ref[...]
        queries = apply_norm(q_ref[0], norms[:, 0:1], norms[:, 1:2], turn)[0]
        keys = apply_norm(k_ref[0], norms[:, 2:3], norms[:, 3:4], turn)[0]
        values = v_ref[0].astype(BF16)
        for start in range(0, queries.shape[1], step):
            part = queries[:, start : start + step]
            scores = masked(dot(keys, part, 0, 0) * (SCALE * LOG2E), limit)
            top = jnp.max(scores, axis=0, keepdims=True)
            weights = jnp.exp2(scores - top)
            total = jnp.sum(weights, axis=0, keepdims=True)
            output = dot(values, weights.astype(BF16))
            out_ref[0, :, start : start + step] = (output / total).astype(BF16)
            log_ref[0, :, start : start + step] = top + jnp.log2(total)

    return body


def attention_backward(rope, step):
    def body(*refs):
        if rope:
            raw_ref, grad_ref, log_ref, norm_ref, cos_ref, sin_ref, out_ref, sums_ref = refs
            q_ref, k_ref, v_ref = (raw_ref.at[i] for i in range(3))
            dq_ref, dk_ref, dv_ref = (out_ref.at[i] for i in range(3))
            turn = (cos_ref[...], sin_ref[...])
            limit = None
        else:
            limit_ref, q_ref, k_ref, v_ref, grad_ref, log_ref, norm_ref = refs[:7]
            dq_ref, dk_ref, dv_ref, sums_ref = refs[7:]
            turn = None
            limit = limit_ref[0] + CLIP
        norms = norm_ref[...]
        queries, q_unit, q_inverse = apply_norm(q_ref[0], norms[:, 0:1], norms[:, 1:2], turn)
        keys, k_unit, k_inverse = apply_norm(k_ref[0], norms[:, 2:3], norms[:, 3:4], turn)
        values = v_ref[0].astype(BF16)
        grads = grad_ref[0]
        logs = log_ref[0]
        query_parts = []
        key_sum = jnp.zeros(keys.shape, F32)
        value_sum = jnp.zeros(keys.shape, F32)
        for start in range(0, queries.shape[1], step):
            part = queries[:, start : start + step]
            grad_part = grads[:, start : start + step]
            scores = masked(dot(keys, part, 0, 0) * (SCALE * LOG2E), limit)
            weights = jnp.exp2(scores - logs[:, start : start + step])
            grad_weights = dot(values, grad_part, 0, 0)
            inner = jnp.sum(weights * grad_weights, axis=0, keepdims=True)
            grad_scores = (weights * (grad_weights - inner)).astype(BF16)
            query_parts.append(dot(keys, grad_scores))
            key_sum = key_sum + dot(part, grad_scores, 1, 1)
            value_sum = value_sum + dot(grad_part, weights.astype(BF16), 1, 1)
        grad_q = (jnp.concatenate(query_parts, axis=1) * SCALE).astype(BF16).astype(F32)
        grad_k = (key_sum * SCALE).astype(BF16).astype(F32)
        raw_q, q_gain, q_offset = norm_back(grad_q, q_unit, q_inverse, norms[:, 0:1], turn)
        raw_k, k_gain, k_offset = norm_back(grad_k, k_unit, k_inverse, norms[:, 2:3], turn)
        dq_ref[0] = raw_q.astype(BF16)
        dk_ref[0] = raw_k.astype(BF16)
        dv_ref[0] = value_sum.astype(BF16)

        @pl.when(pl.program_id(0) == 0)
        def _():
            sums_ref[...] = jnp.zeros(sums_ref.shape, F32)

        for place, terms in enumerate((q_gain, q_offset, k_gain, k_offset)):
            sums_ref[place] += lane_fold(terms)

    return body


def head_spec(width, shift=0):
    return pl.BlockSpec((1, HD, width), lambda h, *_: (h + shift, 0, 0))


def whole_spec(shape):
    return pl.BlockSpec(shape, lambda h, *_: (0,) * len(shape))


def triple_spec(width):
    return pl.BlockSpec((3, 1, HD, width), lambda h: (0, h, 0, 0))


def self_attention(raw, norms, cosine, sine):
    tokens = raw.shape[3]
    return pl.pallas_call(
        attention_forward(True, 256),
        grid=(LOCAL,),
        in_specs=[triple_spec(tokens), whole_spec((HD, 4))]
        + [whole_spec((HD, tokens))] * 2,
        out_specs=[head_spec(tokens), pl.BlockSpec((1, 1, tokens), lambda h: (h, 0, 0))],
        out_shape=[
            jax.ShapeDtypeStruct((LOCAL, HD, tokens), BF16),
            jax.ShapeDtypeStruct((LOCAL, 1, tokens), F32),
        ],
        name="self_forward",
    )(raw, norms, cosine, sine)


def self_attention_back(raw, grads, logs, norms, cosine, sine):
    tokens = raw.shape[3]
    return pl.pallas_call(
        attention_backward(True, 256),
        grid=(LOCAL,),
        in_specs=[triple_spec(tokens), head_spec(tokens)]
        + [pl.BlockSpec((1, 1, tokens), lambda h: (h, 0, 0)), whole_spec((HD, 4))]
        + [whole_spec((HD, tokens))] * 2,
        out_specs=[triple_spec(tokens), whole_spec((4, HD, 128))],
        out_shape=[
            jax.ShapeDtypeStruct((3, LOCAL, HD, tokens), BF16),
            jax.ShapeDtypeStruct((4, HD, 128), F32),
        ],
        name="self_backward",
    )(raw, grads, logs, norms, cosine, sine)


def cross_attention(limit, raw_q, raw_text, norms):
    tokens = raw_q.shape[2]
    slots = raw_text.shape[2]
    return pl.pallas_call(
        attention_forward(False, 512),
        grid_spec=pltpu.PrefetchScalarGridSpec(
            num_scalar_prefetch=1,
            grid=(LOCAL,),
            in_specs=[head_spec(tokens), head_spec(slots), head_spec(slots, LOCAL)]
            + [whole_spec((HD, 4))],
            out_specs=[
                head_spec(tokens),
                pl.BlockSpec((1, 1, tokens), lambda h, *_: (h, 0, 0)),
            ],
        ),
        out_shape=[
            jax.ShapeDtypeStruct((LOCAL, HD, tokens), BF16),
            jax.ShapeDtypeStruct((LOCAL, 1, tokens), F32),
        ],
        name="cross_forward",
    )(limit, raw_q, raw_text, raw_text, norms)


def cross_attention_back(limit, raw_q, raw_text, grads, logs, norms):
    tokens = raw_q.shape[2]
    slots = raw_text.shape[2]
    return pl.pallas_call(
        attention_backward(False, 512),
        grid_spec=pltpu.PrefetchScalarGridSpec(
            num_scalar_prefetch=1,
            grid=(LOCAL,),
            in_specs=[head_spec(tokens), head_spec(slots), head_spec(slots, LOCAL)]
            + [head_spec(tokens), pl.BlockSpec((1, 1, tokens), lambda h, *_: (h, 0, 0))]
            + [whole_spec((HD, 4))],
            out_specs=[head_spec(tokens), head_spec(slots), head_spec(slots)]
            + [whole_spec((4, HD, 128))],
        ),
        out_shape=[
            jax.ShapeDtypeStruct((LOCAL, HD, tokens), BF16),
            jax.ShapeDtypeStruct((LOCAL, HD, slots), BF16),
            jax.ShapeDtypeStruct((LOCAL, HD, slots), BF16),
            jax.ShapeDtypeStruct((4, HD, 128), F32),
        ],
        name="cross_backward",
    )(limit, raw_q, raw_text, raw_text, grads, logs, norms)


def rotary_tables(positions):
    quarter = HD // 4
    frequency = 10000.0 ** (-jnp.arange(quarter, dtype=F32) / quarter)
    rows = (positions // GRID).astype(F32)
    columns = (positions % GRID).astype(F32)
    row_phase = frequency[:, None] * rows[None, :]
    column_phase = frequency[:, None] * columns[None, :]
    phases = jnp.concatenate([row_phase, row_phase, column_phase, column_phase], axis=0)
    signs = jnp.where((jnp.arange(HD) // quarter) % 2 == 0, -1.0, 1.0).astype(F32)
    return jnp.cos(phases), jnp.sin(phases) * signs[:, None]


def shards(
    hidden_in,
    skip_in,
    text,
    temb,
    mt5_len,
    cotangent,
    skip_w,
    time_w,
    qkv_w,
    out_w,
    q2_w,
    kv2_w,
    out2_w,
    fc1_w,
    fc2_w,
    vectors,
    head_norms,
    fc_bias,
):
    chips = lax.axis_size("dp")
    core = lax.axis_index("seq")
    chip = lax.axis_index("dp")
    first_core = core == 0
    half_tokens = hidden_in.shape[1]
    hidden_units = fc_bias.shape[0]
    half_chips = chips // 2
    own_half = (chip // half_chips) == core
    base = jnp.where(own_half, chip, chip ^ masks_of(chips)[-1])
    orders = exchange_orders(chips)
    row_orders = exchange_rows(chips)
    all_chips = jnp.arange(chips, dtype=jnp.int32)
    half_group = jnp.arange(half_chips, dtype=jnp.int32)

    def ordered(mine, other, axis):
        return jnp.where(
            first_core,
            jnp.concatenate([mine, other], axis=axis),
            jnp.concatenate([other, mine], axis=axis),
        )

    def take(value, index, axis):
        return lax.dynamic_index_in_dim(value, index, axis=axis, keepdims=False)

    def both(value):
        return jnp.concatenate([value, core_swap(value)], axis=0)

    def fold(partial):
        arrived = core_swap(partial[half_tokens:].astype(BF16))
        return partial[:half_tokens] + arrived.astype(F32)

    def halves_of(weight, groups):
        parts = weight.reshape(weight.shape[0], groups, 2, -1)
        return (
            take(parts, core, 2).reshape(weight.shape[0], -1),
            take(parts, 1 - core, 2).reshape(weight.shape[0], -1),
        )

    def half_of(vector):
        return take(vector.reshape(vector.shape[:-1] + (2, -1)), core, vector.ndim - 1)

    def spread(half):
        zeros = jnp.zeros_like(half)
        return ordered(half, zeros, half.ndim - 1)

    def columns_item(block, kind):
        return block, orders[kind], None

    def rows_item(block, kind):
        return block, row_orders[kind], own_half

    def assembled(halves, item):
        order, own = item[1:]
        if own is None:
            place = place_of_chip(order, all_chips, chip)
        else:
            place = place_of_chip(order, half_group + half_chips * core, base)
        return assemble(*halves, place)

    def column_order(value, kind):
        halves = reorder(
            value.reshape(chips, -1, value.shape[1]), chip_of_place(orders[kind], chip)
        )
        return [h.reshape(-1, value.shape[1]) for h in halves]

    def row_order(value, kind):
        place = chip_of_place(row_orders[kind], base) - half_chips * core
        halves = reorder(value.reshape(half_chips, -1, value.shape[1]), place)
        return [h.reshape(-1, value.shape[1]) for h in halves]

    def terms_of(left, right, right_dim, blocks):
        return [
            dot(part, right, 1, right_dim).astype(BF16).reshape(blocks // 2, -1, right.shape[1 - right_dim])
            for part in left
        ]

    silu_low = jax.nn.silu(temb).astype(BF16)
    vector_pair = ordered(vectors[None], core_swap(vectors)[None], 0)
    count = vector_pair.size
    own_rows = time_w.shape[0]
    skip_part = skip_w.shape[0]
    own_block = jnp.concatenate([skip_w, time_w, out_w, out2_w], axis=0)
    other_block = core_swap(own_block)

    def row_block(start, size):
        return ordered(own_block[start : start + size], other_block[start : start + size], 0)

    time_start = skip_part
    first_item = rows_item(
        jnp.concatenate([row_block(0, skip_part), row_block(time_start, own_rows)], axis=0), 0
    )
    qkv_own, qkv_other = halves_of(qkv_w, 3)
    qkv_item = columns_item(ordered(qkv_own, core_swap(qkv_other), 0), 1)
    small_item = columns_item(
        jnp.concatenate([vector_pair.reshape(1, -1), silu_low.reshape(1, -1)], axis=1), 0
    )
    first, qkv_halves, small_halves = gather_group([first_item, qkv_item, small_item])
    first = assembled(first, first_item)
    skip_mine = first[:, : 2 * skip_part].reshape(D, D)
    time_mine = first[:, 2 * skip_part :].reshape(HW, D)
    qkv_mine = assembled(qkv_halves, qkv_item).reshape(D, 3 * HW)
    chosen = place_of_chip(small_item[1], all_chips, chip)[:, None] == all_chips[None, :]
    small_all = dot(
        chosen.astype(BF16), jnp.concatenate(small_halves, axis=0).reshape(chips, -1)
    ).astype(BF16)
    vector_full = (
        small_all[:, :count]
        .reshape(chips, 2, vectors.shape[0], -1)
        .transpose(2, 0, 1, 3)
        .reshape(vectors.shape[0], D)
    )
    silu_all = small_all[:, count:]

    q2_own, q2_other = halves_of(q2_w, 1)
    kv_own, kv_other = halves_of(kv2_w, 2)
    kv_part = kv2_w.shape[0]
    four_own = jnp.concatenate([q2_own, kv_own[:, :HW], kv_own[:, HW:]], axis=0)
    four_other = core_swap(jnp.concatenate([q2_other, kv_other[:, :HW], kv_other[:, HW:]], axis=0))
    cuts = (0, own_rows, own_rows + kv_part, own_rows + 2 * kv_part)
    four_item = columns_item(
        jnp.concatenate(
            [ordered(four_own[a:b], four_other[a:b], 0) for a, b in zip(cuts, cuts[1:])], axis=0
        ),
        1,
    )
    pair_item = rows_item(
        jnp.concatenate(
            [row_block(time_start + own_rows, own_rows), row_block(time_start + 2 * own_rows, own_rows)],
            axis=0,
        ),
        0,
    )
    pair, four = gather_group([pair_item, four_item], (first, qkv_halves))
    fc1_own, fc1_other = halves_of(fc1_w, 1)
    fc2_own, fc2_other = halves_of(fc2_w.T, 1)
    fc_other = core_swap(jnp.concatenate([fc1_other, fc2_other], axis=0))
    fc1_item = columns_item(ordered(fc1_own, fc_other[:own_rows], 0), 0)
    fc2_item = columns_item(ordered(fc2_own, fc_other[own_rows:], 0), 1)
    fc1_halves, fc2_halves = gather_group([fc1_item, fc2_item], (pair, four))
    pair = assembled(pair, pair_item)
    out_mine = pair[:, : 2 * own_rows].reshape(HW, D)
    out2_mine = pair[:, 2 * own_rows :].reshape(HW, D)
    four = assembled(four, four_item)
    q2_mine = four[:, : 2 * own_rows].reshape(D, HW)
    k2_mine = four[:, 2 * cuts[1] : 2 * cuts[2]].reshape(-1, HW)
    v2_mine = four[:, 2 * cuts[2] :].reshape(-1, HW)
    fc1_mine = assembled(fc1_halves, fc1_item).reshape(D, -1)
    fc2_mine = assembled(fc2_halves, fc2_item).reshape(D, -1)

    rows = vector_full.astype(F32)
    norms = head_norms.astype(F32)
    norm_columns = norms.T
    hidden = hidden_in[0]
    skipped = skip_in[0]
    own_input = jnp.where(first_core, hidden, skipped)
    joined = jnp.concatenate(
        [own_input, core_swap(jnp.where(first_core, skipped, hidden))], axis=0
    )
    joined_turned = row_order(joined.T, 1)
    skip_other = core_swap(skip_mine)
    hidden_rows = jnp.where(first_core, skip_mine, skip_other)
    skipped_rows = jnp.where(first_core, skip_other, skip_mine)
    grads_all = both(cotangent[0])
    grads_turned = column_order(grads_all.T, 1)
    text_low = jnp.pad(text[0], ((0, TXT_PAD - TXT), (0, 0)))
    text_turned = column_order(text_low.T, 0)
    limit = mt5_len.astype(jnp.int32)
    token = jnp.arange(half_tokens, dtype=jnp.int32)
    positions = jnp.concatenate([core * half_tokens + token, (1 - core) * half_tokens + token])
    cosine, sine = rotary_tables(positions)

    skip_proj = fold(dot(joined, skip_mine)) + rows[0]
    stream_zero = layer_norm(skip_proj, rows[1], rows[2])
    shift_part = dot(half_of(silu_low), time_mine)
    shift = shift_part + core_swap(shift_part) + rows[5]
    attn_in = (layer_norm(stream_zero, rows[3], rows[4]) + shift).astype(BF16)
    attn_all = both(attn_in)
    attn_turned = column_order(attn_all.T, 0)
    raw = dot(qkv_mine, attn_all, 0, 1) + half_of(rows[6:9]).reshape(-1)[:, None]
    raw = raw.reshape(3, LOCAL, HD, -1)
    attended, logs = self_attention(raw, norm_columns[:, :4], cosine, sine)
    attended = attended.reshape(HW, -1)
    stream_one = stream_zero + (fold(dot(attended, out_mine, 0, 0)) + rows[9])
    attended_turned = row_order(attended, 1)
    cross_in = layer_norm(stream_one, rows[10], rows[11]).astype(BF16)
    cross_all = both(cross_in)
    cross_turned = column_order(cross_all.T, 0)
    raw_two = (dot(q2_mine, cross_all, 0, 1) + half_of(rows[12])[:, None]).reshape(LOCAL, HD, -1)
    text_raw = jnp.concatenate(
        [
            dot(k2_mine, text_low, 0, 1) + half_of(rows[13])[:, None],
            dot(v2_mine, text_low, 0, 1) + half_of(rows[14])[:, None],
        ],
        axis=0,
    ).reshape(2 * LOCAL, HD, TXT_PAD)
    crossed, cross_logs = cross_attention(limit, raw_two, text_raw, norm_columns[:, 4:])
    crossed = crossed.reshape(HW, -1)
    stream_two = stream_one + (fold(dot(crossed, out2_mine, 0, 0)) + rows[15])
    crossed_turned = row_order(crossed, 1)
    mlp_in = layer_norm(stream_two, rows[16], rows[17]).astype(BF16)
    mlp_all = both(mlp_in)
    mlp_turned = column_order(mlp_all.T, 0)
    inner_bias = half_of(fc_bias.astype(F32))

    def gelu_tanh(inner):
        return jax.nn.gelu(inner, approximate=True)

    hidden_pre = dot(mlp_all, fc1_mine) + inner_bias
    activated = gelu_tanh(hidden_pre).astype(BF16)
    fc2_terms = terms_of(grads_turned, activated, 0, chips)
    grad_pre = jax.vjp(gelu_tanh, hidden_pre)[1](dot(grads_all, fc2_mine))[0].astype(BF16)
    block_out = stream_two + (fold(dot(activated, fc2_mine, 1, 1)) + rows[18])
    fc1_terms = terms_of(mlp_turned, grad_pre, 0, chips)

    bias_fc2 = column_sum(cotangent[0])
    grad_inner_bias = spread(column_sum(grad_pre))
    grad_mlp_in = fold(dot(grad_pre, fc1_mine, 1, 1))
    norm_pull = jax.vjp(layer_norm, stream_two, rows[16], rows[17])[1]
    from_mlp, gain_two, offset_two = norm_pull(grad_mlp_in)
    grad_two = cotangent[0].astype(F32) + from_mlp

    cross_grad = grad_two.astype(BF16)
    bias_out2 = column_sum(cross_grad)
    cross_grad_all = both(cross_grad)
    grad_crossed = dot(out2_mine, cross_grad_all, 1, 1).astype(BF16).reshape(LOCAL, HD, -1)
    out2_terms = terms_of(crossed_turned, cross_grad_all, 0, half_chips)
    dq2, dk2, dv2, cross_sums = cross_attention_back(
        limit, raw_two, text_raw, grad_crossed, cross_logs, norm_columns[:, 4:]
    )
    dq2 = dq2.reshape(HW, -1)
    dk2 = dk2.reshape(HW, -1)
    dv2 = dv2.reshape(HW, -1)
    four_terms = [
        jnp.concatenate(parts, axis=1)
        for parts in zip(
            terms_of(cross_turned, dq2, 1, chips),
            terms_of(text_turned, dk2, 1, chips),
            terms_of(text_turned, dv2, 1, chips),
        )
    ]
    text_part = dot(dk2, k2_mine, 0, 1) + dot(dv2, v2_mine, 0, 1)
    grad_text = (text_part + core_swap(text_part))[:TXT]
    grad_cross_in = fold(dot(dq2, q2_mine, 0, 1))
    third_pull = jax.vjp(layer_norm, stream_one, rows[10], rows[11])[1]
    from_cross, gain_three, offset_three = third_pull(grad_cross_in)
    grad_one = grad_two + from_cross

    attn_grad = grad_one.astype(BF16)
    bias_out = column_sum(attn_grad)
    attn_grad_all = both(attn_grad)
    grad_attended = dot(out_mine, attn_grad_all, 1, 1).astype(BF16).reshape(LOCAL, HD, -1)
    out_terms = terms_of(attended_turned, attn_grad_all, 0, half_chips)
    qkv_grad, self_sums = self_attention_back(
        raw, grad_attended, logs, norm_columns[:, :4], cosine, sine
    )
    qkv_grad = qkv_grad.reshape(3 * HW, -1)
    grad_attn_in = fold(dot(qkv_grad, qkv_mine, 0, 1))
    qkv_terms = terms_of(attn_turned, qkv_grad, 1, chips)
    first_pull = jax.vjp(layer_norm, stream_zero, rows[3], rows[4])[1]
    from_attn, gain_one, offset_one = first_pull(grad_attn_in)
    grad_zero = grad_one + from_attn
    shift_sum = jnp.sum(grad_attn_in, axis=0, keepdims=True)
    shift_low = (shift_sum + core_swap(shift_sum)).astype(BF16)
    silu_part = dot(shift_low, time_mine, 1, 1)
    silu_grad = ordered(silu_part, core_swap(silu_part), 1)
    grad_temb = jax.vjp(jax.nn.silu, temb)[1](silu_grad)[0]
    device = 2 * chip + core

    skip_pull = jax.vjp(layer_norm, skip_proj, rows[1], rows[2])[1]
    grad_proj, gain_skip, offset_skip = skip_pull(grad_zero)
    proj_low = grad_proj.astype(BF16)
    bias_skip = column_sum(proj_low)
    proj_all = both(proj_low)
    skip_terms = terms_of(joined_turned, proj_all, 0, half_chips)
    grad_hidden = dot(proj_low, hidden_rows, 1, 1)
    grad_skip = dot(proj_low, skipped_rows, 1, 1)

    def split_rows(value, pieces):
        parts = [value[2 * a : 2 * b].reshape(2, b - a, -1) for a, b in zip(pieces, pieces[1:])]
        mine = jnp.concatenate([take(p, core, 0) for p in parts], axis=0)
        other = jnp.concatenate([take(p, 1 - core, 0) for p in parts], axis=0)
        return mine, core_swap(other)

    def column_results(value, pieces, groups=1):
        mine, other = (
            part.reshape(part.shape[0], groups, 1, -1) for part in split_rows(value, pieces)
        )
        whole = ordered(mine, other, 2).reshape(mine.shape[0], -1)
        return [whole[a:b] for a, b in zip(pieces, pieces[1:])]

    def row_results(value, pieces):
        mine, other = split_rows(value, pieces)
        whole = jnp.where(own_half, mine, other)
        return [whole[a:b] for a, b in zip(pieces, pieces[1:])]

    after_cross = dq2
    after_one = attn_grad
    after_self = qkv_grad
    after_attn = grad_attn_in
    after_proj = proj_low
    fc1_grad, fc2_grad = scatter_group(
        [(*fc1_terms, orders[0], False), (*fc2_terms, orders[1], False)],
        (after_cross, after_one, after_self, after_attn),
    )
    grad_fc1, grad_fc2 = column_results(
        jnp.concatenate([fc1_grad, fc2_grad], axis=0), (0, own_rows, 2 * own_rows)
    )
    grad_fc2 = grad_fc2.T
    pair_terms = [jnp.concatenate(parts, axis=1) for parts in zip(out_terms, out2_terms)]
    four_grad, pair_grad = scatter_group(
        [(*four_terms, orders[0], False), (*pair_terms, row_orders[1], True)],
        (after_self, after_attn, after_proj),
    )
    four_results = column_results(four_grad, cuts)
    grad_q2 = four_results[0]
    grad_kv2 = jnp.concatenate(four_results[1:], axis=1)
    grad_out, grad_out2 = row_results(pair_grad, (0, own_rows, 2 * own_rows))
    (qkv_result,) = scatter_group([(*qkv_terms, orders[0], False)], (after_proj,))
    (grad_qkv,) = column_results(qkv_result, (0, own_rows), 3)
    (skip_result,) = scatter_group([(*skip_terms, row_orders[1], True)])
    (grad_skipw,) = row_results(skip_result, (0, skip_part))

    def bias_of(grads):
        return spread(column_sum(grads, axis=1).reshape(-1, HW))

    bias_qkv = bias_of(qkv_grad)
    owner = first_core.astype(F32)
    vector_grad = jnp.stack(
        [
            bias_skip,
            gain_skip,
            offset_skip,
            gain_one,
            offset_one,
            shift_low[0].astype(F32) * owner,
            bias_qkv[0],
            bias_qkv[1],
            bias_qkv[2],
            bias_out,
            gain_three,
            offset_three,
            bias_of(dq2)[0],
            bias_of(dk2)[0],
            bias_of(dv2)[0],
            bias_out2,
            gain_two,
            offset_two,
            bias_fc2,
        ]
    )
    norm_grad = jnp.concatenate([jnp.sum(self_sums, axis=2), jnp.sum(cross_sums, axis=2)])
    shift_rows = jnp.where(all_chips[:, None] == chip, shift_low.astype(F32), 0.0) * owner
    packed = jnp.concatenate(
        [x.reshape(-1) for x in (vector_grad, norm_grad, grad_inner_bias, shift_rows)]
    )
    packed = packed + core_swap(packed)
    for move in masks_of(chips):
        packed = packed + chip_swap(packed, (move, move))
    vector_count = vector_grad.size
    norm_count = norm_grad.size
    vector_here = vectors.shape[1]
    grad_vectors = lax.dynamic_slice_in_dim(
        packed[:vector_count].reshape(vector_grad.shape), device * vector_here, vector_here, axis=1
    )
    norm_total = packed[vector_count : vector_count + norm_count].reshape(norm_grad.shape)
    bias_end = vector_count + norm_count + hidden_units
    bias_total = packed[vector_count + norm_count : bias_end]
    shift_all = packed[bias_end:].reshape(chips, D).astype(BF16)
    silu_here = lax.dynamic_slice_in_dim(silu_all, device * own_rows, own_rows, axis=1)
    grad_time = dot(silu_here, shift_all, 0, 0)
    return (
        block_out[None],
        grad_hidden[None],
        grad_skip[None],
        grad_text[None],
        grad_temb,
        grad_skipw,
        grad_time,
        grad_qkv,
        grad_out,
        grad_q2,
        grad_kv2,
        grad_out2,
        grad_fc1,
        grad_fc2,
        grad_vectors,
        norm_total,
        bias_total,
    )


def solution(mesh):
    tokens = P("dp", "seq", None)
    rows = P(AXES, None)
    columns = P(None, AXES)
    return jax.shard_map(
        shards,
        mesh=mesh,
        in_specs=(
            tokens,
            tokens,
            P("dp", None, None),
            P("dp", None),
            P("dp"),
            tokens,
            rows,
            rows,
            rows,
            rows,
            rows,
            rows,
            rows,
            rows,
            columns,
            columns,
            P(),
            P(),
        ),
        out_specs=(
            tokens,
            tokens,
            tokens,
            P("dp", None, None),
            P("dp", None),
            rows,
            rows,
            rows,
            rows,
            rows,
            rows,
            rows,
            rows,
            columns,
            columns,
            P(),
            P(),
        ),
        check_vma=False,
    )
```

```python
import math

import jax
import jax.numpy as jnp
from jax import lax
from jax.experimental import pallas as pl
from jax.experimental.pallas import tpu as pltpu
from jax.sharding import PartitionSpec as P

D = 1408
HEADS = 16
CLIP = 77
GRID = 32
HD = 88
TXT = 333
TXT_PAD = 384
LOCAL = HEADS // 2
HW = LOCAL * HD
AXES = ("dp", "seq")
SCALE = HD**-0.5
LOG2E = math.log2(math.e)

EPSILON = 1e-06

F32 = jnp.float32
BF16 = jnp.bfloat16


def layer_norm(inputs, scales, offset):
    middle = jnp.mean(inputs, axis=-1, keepdims=True)
    centred = inputs - middle
    variance = jnp.mean(centred * centred, axis=-1, keepdims=True)
    return centred * lax.rsqrt(variance + EPSILON) * scales + offset


def dot(left, right, left_dim=1, right_dim=0):
    return lax.dot_general(
        left, right, (((left_dim,), (right_dim,)), ((), ())), preferred_element_type=F32
    )


def column_sum(inputs, axis=0):
    return jnp.sum(inputs.astype(F32), axis=axis)


def core_swap(value):
    chips = lax.axis_size("dp")
    pairs = [(2 * i + s, 2 * i + 1 - s) for i in range(chips) for s in range(2)]
    return lax.ppermute(value, AXES, pairs)


def masks_of(chips):
    if chips == 16:
        return (1, 2, 4, 12)
    if chips == 64:
        return (1, 3, 4, 12, 16, 48)
    return tuple(1 << b for b in range(chips.bit_length() - 1))


def exchange_orders(chips):
    moves = masks_of(chips)
    half = len(moves) // 2
    first, second = moves[:half], moves[half:]
    return (
        (first + second, second + first),
        (first[::-1] + second[::-1], second[::-1] + first[::-1]),
    )


def exchange_rows(chips):
    moves = masks_of(chips)[:-1]
    return (
        (moves, moves[-1:] + moves[:-1]),
        (moves[1:] + moves[:1], moves[1:-1] + moves[-1:] + moves[:1]),
    )


def chip_swap(value, moves):
    chips = lax.axis_size("dp")
    pairs = [(2 * i + s, 2 * (i ^ moves[s]) + s) for i in range(chips) for s in range(2)]
    return lax.ppermute(value, AXES, pairs)


def chip_send(value, from_own):
    chips = lax.axis_size("dp")
    move = masks_of(chips)[-1]
    pairs = [
        (2 * i + s, 2 * (i ^ move) + s)
        for i in range(chips)
        for s in range(2)
        if ((2 * i // chips) == s) == from_own
    ]
    return lax.ppermute(value, AXES, pairs)


def tie(value, milestone):
    return value if milestone is None else lax.optimization_barrier((value, milestone))[0]


def chip_of_place(order, base):
    count = len(order[0])
    place = jnp.arange(1 << count, dtype=jnp.int32)
    chip = [base + jnp.zeros_like(place) for _ in range(2)]
    for step in range(count):
        bit = (place >> (count - 1 - step)) & 1
        chip = [c ^ (bit * o[step]) for c, o in zip(chip, order)]
    return jnp.where(lax.axis_index("seq") == 0, chip[0], chip[1])


def place_of_chip(order, target, base):
    count = len(order[0])
    both_cores = []
    for moves in order:
        columns = {}
        for code in range(1 << count):
            mask = 0
            for step in range(count):
                if (code >> (count - 1 - step)) & 1:
                    mask ^= moves[step]
            columns[mask] = code
        difference = target ^ base
        place = jnp.zeros_like(difference)
        for bit in range(max(columns).bit_length()):
            place = place ^ (((difference >> bit) & 1) * columns[1 << bit])
        both_cores.append(place)
    return jnp.where(lax.axis_index("seq") == 0, both_cores[0], both_cores[1])


def gather_group(items, after=None):
    values = [block[None] for block, _, _ in items]
    steps = [len(order[0]) + (own is not None) for _, order, own in items]
    others = [None] * len(items)
    if after is not None:
        values = list(lax.optimization_barrier((tuple(values), after))[0])
    for step in range(max(steps)):
        for i, (_, order, own) in enumerate(items):
            if own is not None and step == 0:
                others[i] = chip_send(values[i], True)
            else:
                move = steps[i] - 1 - step
                others[i] = chip_swap(values[i], (order[0][move], order[1][move]))
        values, others = (
            list(part) for part in lax.optimization_barrier((tuple(values), tuple(others)))
        )
        if step == max(steps) - 1:
            break
        for i, (_, _, own) in enumerate(items):
            if own is not None and step == 0:
                values[i] = jnp.where(own, values[i], others[i])
            else:
                values[i] = jnp.concatenate([values[i], others[i]], axis=0)
    return list(zip(values, others))


def scatter_group(items, ties=()):
    sources = [[kept] for kept, _, _, _ in items]
    leaving = [leave for _, leave, _, _ in items]
    count = max(len(order[0]) + rows for _, _, order, rows in items)
    for step in range(count):
        arrived = []
        for i, (_, _, order, rows) in enumerate(items):
            if rows and step == len(order[0]):
                arrived.append(chip_send(leaving[i], False))
            else:
                arrived.append(chip_swap(leaving[i], (order[0][step], order[1][step])))
        milestone = ties[step] if step < len(ties) else ()
        arrived = lax.optimization_barrier((tuple(arrived), milestone))[0]
        for i, (_, _, order, rows) in enumerate(items):
            sources[i].append(arrived[i])
            if step + 1 < len(order[0]):
                half = sources[i][0].shape[0] // 2
                leaving[i] = sum(s[half:].astype(F32) for s in sources[i]).astype(BF16)
                sources[i] = [s[:half] for s in sources[i]]
            elif step + 1 < count:
                total = sum(s.astype(F32) for s in sources[i])
                leaving[i] = total.astype(BF16)
                sources[i] = [total]
    return [sum(s.astype(F32) for s in terms)[0] for terms in sources]


def assemble(lower, upper, index):
    half = lower.shape[0]
    count = index.shape[0]

    def body(index_ref, lower_ref, upper_ref, out_ref, sems):
        for j in range(count):
            source = index_ref[j]

            @pl.when(source < half)
            def _():
                pltpu.make_async_copy(lower_ref.at[source], out_ref.at[j], sems.at[j]).start()

            @pl.when(source >= half)
            def _():
                pltpu.make_async_copy(
                    upper_ref.at[source - half], out_ref.at[j], sems.at[j]
                ).start()

        for j in range(count):
            pltpu.make_async_copy(lower_ref.at[0], out_ref.at[j], sems.at[j]).wait()

    shape = (count,) + lower.shape[1:]
    return pl.pallas_call(
        body,
        grid_spec=pltpu.PrefetchScalarGridSpec(
            num_scalar_prefetch=1,
            grid=(1,),
            in_specs=[pl.BlockSpec(memory_space=pl.ANY)] * 2,
            out_specs=pl.BlockSpec(shape, lambda i, *_: (0, 0, 0)),
            scratch_shapes=[pltpu.SemaphoreType.DMA((count,))],
        ),
        out_shape=jax.ShapeDtypeStruct(shape, lower.dtype),
        name="assemble",
    )(index, lower, upper)


def reorder(value, index):
    count = index.shape[0]
    half = count // 2
    shape = (half,) + value.shape[1:]

    def body(index_ref, value_ref, lower_ref, upper_ref, sems):
        places = [lower_ref.at[j] for j in range(half)] + [upper_ref.at[j] for j in range(half)]
        for j, place in enumerate(places):
            pltpu.make_async_copy(value_ref.at[index_ref[j]], place, sems.at[j]).start()
        for j, place in enumerate(places):
            pltpu.make_async_copy(value_ref.at[0], place, sems.at[j]).wait()

    return pl.pallas_call(
        body,
        grid_spec=pltpu.PrefetchScalarGridSpec(
            num_scalar_prefetch=1,
            grid=(1,),
            in_specs=[pl.BlockSpec(memory_space=pl.ANY)],
            out_specs=[pl.BlockSpec(shape, lambda i, *_: (0, 0, 0))] * 2,
            scratch_shapes=[pltpu.SemaphoreType.DMA((count,))],
        ),
        out_shape=[jax.ShapeDtypeStruct(shape, value.dtype)] * 2,
        name="reorder",
    )(index, value)


def swap_groups(value):
    quarter = HD // 4
    return jnp.concatenate(
        [
            value[quarter : 2 * quarter],
            value[:quarter],
            value[3 * quarter :],
            value[2 * quarter : 3 * quarter],
        ],
        axis=0,
    )


def normalised(raw):
    middle = jnp.sum(raw, axis=0, keepdims=True) * (1.0 / HD)
    centred = raw - middle
    variance = jnp.sum(centred * centred, axis=0, keepdims=True) * (1.0 / HD)
    inverse = lax.rsqrt(variance + EPSILON)
    return centred * inverse, inverse


def apply_norm(raw, gain, offset, turn):
    unit, inverse = normalised(raw)
    value = unit * gain + offset
    if turn is not None:
        value = value * turn[0] + swap_groups(value) * turn[1]
    return value.astype(BF16), unit, inverse


def norm_back(grad, unit, inverse, gain, turn):
    if turn is not None:
        grad = grad * turn[0] + swap_groups(grad * turn[1])
    gain_terms = grad * unit
    inner = grad * gain
    mean_one = jnp.sum(inner, axis=0, keepdims=True) * (1.0 / HD)
    mean_two = jnp.sum(inner * unit, axis=0, keepdims=True) * (1.0 / HD)
    return inverse * (inner - mean_one - unit * mean_two), gain_terms, grad


def lane_fold(value):
    lanes = value.shape[1]
    return sum(value[:, i : i + 128] for i in range(0, lanes, 128))


def masked(scores, limit):
    if limit is None:
        return scores
    index = lax.broadcasted_iota(jnp.int32, scores.shape, 0)
    return jnp.where(index < limit, scores, -1e30)


def attention_forward(rope, step):
    def body(*refs):
        if rope:
            raw_ref, norm_ref, cos_ref, sin_ref, out_ref, log_ref = refs
            q_ref, k_ref, v_ref = (raw_ref.at[i] for i in range(3))
            turn = (cos_ref[...], sin_ref[...])
            limit = None
        else:
            limit_ref, q_ref, k_ref, v_ref, norm_ref, out_ref, log_ref = refs
            turn = None
            limit = limit_ref[0] + CLIP
        norms = norm_ref[...]
        queries = apply_norm(q_ref[0], norms[:, 0:1], norms[:, 1:2], turn)[0]
        keys = apply_norm(k_ref[0], norms[:, 2:3], norms[:, 3:4], turn)[0]
        values = v_ref[0].astype(BF16)
        for start in range(0, queries.shape[1], step):
            part = queries[:, start : start + step]
            scores = masked(dot(keys, part, 0, 0) * (SCALE * LOG2E), limit)
            top = jnp.max(scores, axis=0, keepdims=True)
            weights = jnp.exp2(scores - top)
            total = jnp.sum(weights, axis=0, keepdims=True)
            output = dot(values, weights.astype(BF16))
            out_ref[0, :, start : start + step] = (output / total).astype(BF16)
            log_ref[0, :, start : start + step] = top + jnp.log2(total)

    return body


def attention_backward(rope, step):
    def body(*refs):
        if rope:
            raw_ref, grad_ref, log_ref, norm_ref, cos_ref, sin_ref, out_ref, sums_ref = refs
            q_ref, k_ref, v_ref = (raw_ref.at[i] for i in range(3))
            dq_ref, dk_ref, dv_ref = (out_ref.at[i] for i in range(3))
            turn = (cos_ref[...], sin_ref[...])
            limit = None
        else:
            limit_ref, q_ref, k_ref, v_ref, grad_ref, log_ref, norm_ref = refs[:7]
            dq_ref, dk_ref, dv_ref, sums_ref = refs[7:]
            turn = None
            limit = limit_ref[0] + CLIP
        norms = norm_ref[...]
        queries, q_unit, q_inverse = apply_norm(q_ref[0], norms[:, 0:1], norms[:, 1:2], turn)
        keys, k_unit, k_inverse = apply_norm(k_ref[0], norms[:, 2:3], norms[:, 3:4], turn)
        values = v_ref[0].astype(BF16)
        grads = grad_ref[0]
        logs = log_ref[0]
        query_parts = []
        key_sum = jnp.zeros(keys.shape, F32)
        value_sum = jnp.zeros(keys.shape, F32)
        for start in range(0, queries.shape[1], step):
            part = queries[:, start : start + step]
            grad_part = grads[:, start : start + step]
            scores = masked(dot(keys, part, 0, 0) * (SCALE * LOG2E), limit)
            weights = jnp.exp2(scores - logs[:, start : start + step])
            grad_weights = dot(values, grad_part, 0, 0)
            inner = jnp.sum(weights * grad_weights, axis=0, keepdims=True)
            grad_scores = (weights * (grad_weights - inner)).astype(BF16)
            query_parts.append(dot(keys, grad_scores))
            key_sum = key_sum + dot(part, grad_scores, 1, 1)
            value_sum = value_sum + dot(grad_part, weights.astype(BF16), 1, 1)
        grad_q = (jnp.concatenate(query_parts, axis=1) * SCALE).astype(BF16).astype(F32)
        grad_k = (key_sum * SCALE).astype(BF16).astype(F32)
        raw_q, q_gain, q_offset = norm_back(grad_q, q_unit, q_inverse, norms[:, 0:1], turn)
        raw_k, k_gain, k_offset = norm_back(grad_k, k_unit, k_inverse, norms[:, 2:3], turn)
        dq_ref[0] = raw_q.astype(BF16)
        dk_ref[0] = raw_k.astype(BF16)
        dv_ref[0] = value_sum.astype(BF16)

        @pl.when(pl.program_id(0) == 0)
        def _():
            sums_ref[...] = jnp.zeros(sums_ref.shape, F32)

        for place, terms in enumerate((q_gain, q_offset, k_gain, k_offset)):
            sums_ref[place] += lane_fold(terms)

    return body


def head_spec(width, shift=0):
    return pl.BlockSpec((1, HD, width), lambda h, *_: (h + shift, 0, 0))


def whole_spec(shape):
    return pl.BlockSpec(shape, lambda h, *_: (0,) * len(shape))


def triple_spec(width):
    return pl.BlockSpec((3, 1, HD, width), lambda h: (0, h, 0, 0))


def self_attention(raw, norms, cosine, sine):
    tokens = raw.shape[3]
    return pl.pallas_call(
        attention_forward(True, 256),
        grid=(LOCAL,),
        in_specs=[triple_spec(tokens), whole_spec((HD, 4))]
        + [whole_spec((HD, tokens))] * 2,
        out_specs=[head_spec(tokens), pl.BlockSpec((1, 1, tokens), lambda h: (h, 0, 0))],
        out_shape=[
            jax.ShapeDtypeStruct((LOCAL, HD, tokens), BF16),
            jax.ShapeDtypeStruct((LOCAL, 1, tokens), F32),
        ],
        name="self_forward",
    )(raw, norms, cosine, sine)


def self_attention_back(raw, grads, logs, norms, cosine, sine):
    tokens = raw.shape[3]
    return pl.pallas_call(
        attention_backward(True, 256),
        grid=(LOCAL,),
        in_specs=[triple_spec(tokens), head_spec(tokens)]
        + [pl.BlockSpec((1, 1, tokens), lambda h: (h, 0, 0)), whole_spec((HD, 4))]
        + [whole_spec((HD, tokens))] * 2,
        out_specs=[triple_spec(tokens), whole_spec((4, HD, 128))],
        out_shape=[
            jax.ShapeDtypeStruct((3, LOCAL, HD, tokens), BF16),
            jax.ShapeDtypeStruct((4, HD, 128), F32),
        ],
        name="self_backward",
    )(raw, grads, logs, norms, cosine, sine)


def cross_attention(limit, raw_q, raw_text, norms):
    tokens = raw_q.shape[2]
    slots = raw_text.shape[2]
    return pl.pallas_call(
        attention_forward(False, 512),
        grid_spec=pltpu.PrefetchScalarGridSpec(
            num_scalar_prefetch=1,
            grid=(LOCAL,),
            in_specs=[head_spec(tokens), head_spec(slots), head_spec(slots, LOCAL)]
            + [whole_spec((HD, 4))],
            out_specs=[
                head_spec(tokens),
                pl.BlockSpec((1, 1, tokens), lambda h, *_: (h, 0, 0)),
            ],
        ),
        out_shape=[
            jax.ShapeDtypeStruct((LOCAL, HD, tokens), BF16),
            jax.ShapeDtypeStruct((LOCAL, 1, tokens), F32),
        ],
        name="cross_forward",
    )(limit, raw_q, raw_text, raw_text, norms)


def cross_attention_back(limit, raw_q, raw_text, grads, logs, norms):
    tokens = raw_q.shape[2]
    slots = raw_text.shape[2]
    return pl.pallas_call(
        attention_backward(False, 512),
        grid_spec=pltpu.PrefetchScalarGridSpec(
            num_scalar_prefetch=1,
            grid=(LOCAL,),
            in_specs=[head_spec(tokens), head_spec(slots), head_spec(slots, LOCAL)]
            + [head_spec(tokens), pl.BlockSpec((1, 1, tokens), lambda h, *_: (h, 0, 0))]
            + [whole_spec((HD, 4))],
            out_specs=[head_spec(tokens), head_spec(slots), head_spec(slots)]
            + [whole_spec((4, HD, 128))],
        ),
        out_shape=[
            jax.ShapeDtypeStruct((LOCAL, HD, tokens), BF16),
            jax.ShapeDtypeStruct((LOCAL, HD, slots), BF16),
            jax.ShapeDtypeStruct((LOCAL, HD, slots), BF16),
            jax.ShapeDtypeStruct((4, HD, 128), F32),
        ],
        name="cross_backward",
    )(limit, raw_q, raw_text, raw_text, grads, logs, norms)


def rotary_tables(positions):
    quarter = HD // 4
    frequency = 10000.0 ** (-jnp.arange(quarter, dtype=F32) / quarter)
    rows = (positions // GRID).astype(F32)
    columns = (positions % GRID).astype(F32)
    row_phase = frequency[:, None] * rows[None, :]
    column_phase = frequency[:, None] * columns[None, :]
    phases = jnp.concatenate([row_phase, row_phase, column_phase, column_phase], axis=0)
    signs = jnp.where((jnp.arange(HD) // quarter) % 2 == 0, -1.0, 1.0).astype(F32)
    return jnp.cos(phases), jnp.sin(phases) * signs[:, None]


def shards(
    hidden_in,
    skip_in,
    text,
    temb,
    mt5_len,
    cotangent,
    skip_w,
    time_w,
    qkv_w,
    out_w,
    q2_w,
    kv2_w,
    out2_w,
    fc1_w,
    fc2_w,
    vectors,
    head_norms,
    fc_bias,
):
    chips = lax.axis_size("dp")
    core = lax.axis_index("seq")
    chip = lax.axis_index("dp")
    first_core = core == 0
    half_tokens = hidden_in.shape[1]
    hidden_units = fc_bias.shape[0]
    half_chips = chips // 2
    own_half = (chip // half_chips) == core
    base = jnp.where(own_half, chip, chip ^ masks_of(chips)[-1])
    orders = exchange_orders(chips)
    row_orders = exchange_rows(chips)
    all_chips = jnp.arange(chips, dtype=jnp.int32)
    half_group = jnp.arange(half_chips, dtype=jnp.int32)

    def ordered(mine, other, axis):
        return jnp.where(
            first_core,
            jnp.concatenate([mine, other], axis=axis),
            jnp.concatenate([other, mine], axis=axis),
        )

    def take(value, index, axis):
        return lax.dynamic_index_in_dim(value, index, axis=axis, keepdims=False)

    def both(value):
        return jnp.concatenate([value, core_swap(value)], axis=0)

    def fold(partial):
        arrived = core_swap(partial[half_tokens:].astype(BF16))
        return partial[:half_tokens] + arrived.astype(F32)

    def halves_of(weight, groups):
        parts = weight.reshape(weight.shape[0], groups, 2, -1)
        return (
            take(parts, core, 2).reshape(weight.shape[0], -1),
            take(parts, 1 - core, 2).reshape(weight.shape[0], -1),
        )

    def half_of(vector):
        return take(vector.reshape(vector.shape[:-1] + (2, -1)), core, vector.ndim - 1)

    def spread(half):
        zeros = jnp.zeros_like(half)
        return ordered(half, zeros, half.ndim - 1)

    def columns_item(block, kind):
        return block, orders[kind], None

    def rows_item(block, kind):
        return block, row_orders[kind], own_half

    def assembled(halves, item):
        order, own = item[1:]
        if own is None:
            place = place_of_chip(order, all_chips, chip)
        else:
            place = place_of_chip(order, half_group + half_chips * core, base)
        return assemble(*halves, place)

    def column_order(value, kind):
        halves = reorder(
            value.reshape(chips, -1, value.shape[1]), chip_of_place(orders[kind], chip)
        )
        return [h.reshape(-1, value.shape[1]) for h in halves]

    def row_order(value, kind):
        place = chip_of_place(row_orders[kind], base) - half_chips * core
        halves = reorder(value.reshape(half_chips, -1, value.shape[1]), place)
        return [h.reshape(-1, value.shape[1]) for h in halves]

    def terms_of(left, right, right_dim, blocks):
        return [
            dot(part, right, 1, right_dim).astype(BF16).reshape(blocks // 2, -1, right.shape[1 - right_dim])
            for part in left
        ]

    silu_low = jax.nn.silu(temb).astype(BF16)
    vector_pair = ordered(vectors[None], core_swap(vectors)[None], 0)
    count = vector_pair.size
    own_rows = time_w.shape[0]
    skip_part = skip_w.shape[0]
    own_block = jnp.concatenate([skip_w, time_w, out_w, out2_w], axis=0)
    other_block = core_swap(own_block)

    def row_block(start, size):
        return ordered(own_block[start : start + size], other_block[start : start + size], 0)

    time_start = skip_part
    first_item = rows_item(
        jnp.concatenate([row_block(0, skip_part), row_block(time_start, own_rows)], axis=0), 0
    )
    qkv_own, qkv_other = halves_of(qkv_w, 3)
    qkv_item = columns_item(ordered(qkv_own, core_swap(qkv_other), 0), 1)
    small_item = columns_item(
        jnp.concatenate([vector_pair.reshape(1, -1), silu_low.reshape(1, -1)], axis=1), 0
    )
    first, qkv_halves, small_halves = gather_group([first_item, qkv_item, small_item])
    first = assembled(first, first_item)
    skip_mine = first[:, : 2 * skip_part].reshape(D, D)
    time_mine = first[:, 2 * skip_part :].reshape(HW, D)
    qkv_mine = assembled(qkv_halves, qkv_item).reshape(D, 3 * HW)
    chosen = place_of_chip(small_item[1], all_chips, chip)[:, None] == all_chips[None, :]
    small_all = dot(
        chosen.astype(BF16), jnp.concatenate(small_halves, axis=0).reshape(chips, -1)
    ).astype(BF16)
    vector_full = (
        small_all[:, :count]
        .reshape(chips, 2, vectors.shape[0], -1)
        .transpose(2, 0, 1, 3)
        .reshape(vectors.shape[0], D)
    )
    silu_all = small_all[:, count:]

    q2_own, q2_other = halves_of(q2_w, 1)
    kv_own, kv_other = halves_of(kv2_w, 2)
    kv_part = kv2_w.shape[0]
    four_own = jnp.concatenate([q2_own, kv_own[:, :HW], kv_own[:, HW:]], axis=0)
    four_other = core_swap(jnp.concatenate([q2_other, kv_other[:, :HW], kv_other[:, HW:]], axis=0))
    cuts = (0, own_rows, own_rows + kv_part, own_rows + 2 * kv_part)
    four_item = columns_item(
        jnp.concatenate(
            [ordered(four_own[a:b], four_other[a:b], 0) for a, b in zip(cuts, cuts[1:])], axis=0
        ),
        1,
    )
    pair_item = rows_item(
        jnp.concatenate(
            [row_block(time_start + own_rows, own_rows), row_block(time_start + 2 * own_rows, own_rows)],
            axis=0,
        ),
        0,
    )
    pair, four = gather_group([pair_item, four_item], (first, qkv_halves))
    fc1_own, fc1_other = halves_of(fc1_w, 1)
    fc2_own, fc2_other = halves_of(fc2_w.T, 1)
    fc_other = core_swap(jnp.concatenate([fc1_other, fc2_other], axis=0))
    fc1_item = columns_item(ordered(fc1_own, fc_other[:own_rows], 0), 0)
    fc2_item = columns_item(ordered(fc2_own, fc_other[own_rows:], 0), 1)
    fc1_halves, fc2_halves = gather_group([fc1_item, fc2_item], (pair, four))
    pair = assembled(pair, pair_item)
    out_mine = pair[:, : 2 * own_rows].reshape(HW, D)
    out2_mine = pair[:, 2 * own_rows :].reshape(HW, D)
    four = assembled(four, four_item)
    q2_mine = four[:, : 2 * own_rows].reshape(D, HW)
    k2_mine = four[:, 2 * cuts[1] : 2 * cuts[2]].reshape(-1, HW)
    v2_mine = four[:, 2 * cuts[2] :].reshape(-1, HW)
    fc1_mine = assembled(fc1_halves, fc1_item).reshape(D, -1)
    fc2_mine = assembled(fc2_halves, fc2_item).reshape(D, -1)

    rows = vector_full.astype(F32)
    norms = head_norms.astype(F32)
    norm_columns = norms.T
    hidden = hidden_in[0]
    skipped = skip_in[0]
    own_input = jnp.where(first_core, hidden, skipped)
    joined = jnp.concatenate(
        [own_input, core_swap(jnp.where(first_core, skipped, hidden))], axis=0
    )
    joined_turned = row_order(joined.T, 1)
    skip_other = core_swap(skip_mine)
    hidden_rows = jnp.where(first_core, skip_mine, skip_other)
    skipped_rows = jnp.where(first_core, skip_other, skip_mine)
    grads_all = both(cotangent[0])
    grads_turned = column_order(grads_all.T, 1)
    text_low = jnp.pad(text[0], ((0, TXT_PAD - TXT), (0, 0)))
    text_turned = column_order(text_low.T, 0)
    limit = mt5_len.astype(jnp.int32)
    token = jnp.arange(half_tokens, dtype=jnp.int32)
    positions = jnp.concatenate([core * half_tokens + token, (1 - core) * half_tokens + token])
    cosine, sine = rotary_tables(positions)

    skip_proj = fold(dot(joined, skip_mine)) + rows[0]
    stream_zero = layer_norm(skip_proj, rows[1], rows[2])
    shift_part = dot(half_of(silu_low), time_mine)
    shift = shift_part + core_swap(shift_part) + rows[5]
    attn_in = (layer_norm(stream_zero, rows[3], rows[4]) + shift).astype(BF16)
    attn_all = both(attn_in)
    attn_turned = column_order(attn_all.T, 0)
    raw = dot(qkv_mine, attn_all, 0, 1) + half_of(rows[6:9]).reshape(-1)[:, None]
    raw = raw.reshape(3, LOCAL, HD, -1)
    attended, logs = self_attention(raw, norm_columns[:, :4], cosine, sine)
    attended = attended.reshape(HW, -1)
    stream_one = stream_zero + (fold(dot(attended, out_mine, 0, 0)) + rows[9])
    attended_turned = row_order(attended, 1)
    cross_in = layer_norm(stream_one, rows[10], rows[11]).astype(BF16)
    cross_all = both(cross_in)
    cross_turned = column_order(cross_all.T, 0)
    raw_two = (dot(q2_mine, cross_all, 0, 1) + half_of(rows[12])[:, None]).reshape(LOCAL, HD, -1)
    text_raw = jnp.concatenate(
        [
            dot(k2_mine, text_low, 0, 1) + half_of(rows[13])[:, None],
            dot(v2_mine, text_low, 0, 1) + half_of(rows[14])[:, None],
        ],
        axis=0,
    ).reshape(2 * LOCAL, HD, TXT_PAD)
    crossed, cross_logs = cross_attention(limit, raw_two, text_raw, norm_columns[:, 4:])
    crossed = crossed.reshape(HW, -1)
    stream_two = stream_one + (fold(dot(crossed, out2_mine, 0, 0)) + rows[15])
    crossed_turned = row_order(crossed, 1)
    mlp_in = layer_norm(stream_two, rows[16], rows[17]).astype(BF16)
    mlp_all = both(mlp_in)
    mlp_turned = column_order(mlp_all.T, 0)
    inner_bias = half_of(fc_bias.astype(F32))

    def gelu_tanh(inner):
        return jax.nn.gelu(inner, approximate=True)

    hidden_pre = dot(mlp_all, fc1_mine) + inner_bias
    activated = gelu_tanh(hidden_pre).astype(BF16)
    fc2_terms = terms_of(grads_turned, activated, 0, chips)
    grad_pre = jax.vjp(gelu_tanh, hidden_pre)[1](dot(grads_all, fc2_mine))[0].astype(BF16)
    block_out = stream_two + (fold(dot(activated, fc2_mine, 1, 1)) + rows[18])
    fc1_terms = terms_of(mlp_turned, grad_pre, 0, chips)

    bias_fc2 = column_sum(cotangent[0])
    grad_inner_bias = spread(column_sum(grad_pre))
    grad_mlp_in = fold(dot(grad_pre, fc1_mine, 1, 1))
    norm_pull = jax.vjp(layer_norm, stream_two, rows[16], rows[17])[1]
    from_mlp, gain_two, offset_two = norm_pull(grad_mlp_in)
    grad_two = cotangent[0].astype(F32) + from_mlp

    cross_grad = grad_two.astype(BF16)
    bias_out2 = column_sum(cross_grad)
    cross_grad_all = both(cross_grad)
    grad_crossed = dot(out2_mine, cross_grad_all, 1, 1).astype(BF16).reshape(LOCAL, HD, -1)
    out2_terms = terms_of(crossed_turned, cross_grad_all, 0, half_chips)
    dq2, dk2, dv2, cross_sums = cross_attention_back(
        limit, raw_two, text_raw, grad_crossed, cross_logs, norm_columns[:, 4:]
    )
    dq2 = dq2.reshape(HW, -1)
    dk2 = dk2.reshape(HW, -1)
    dv2 = dv2.reshape(HW, -1)
    four_terms = [
        jnp.concatenate(parts, axis=1)
        for parts in zip(
            terms_of(cross_turned, dq2, 1, chips),
            terms_of(text_turned, dk2, 1, chips),
            terms_of(text_turned, dv2, 1, chips),
        )
    ]
    text_part = dot(dk2, k2_mine, 0, 1) + dot(dv2, v2_mine, 0, 1)
    grad_text = (text_part + core_swap(text_part))[:TXT]
    grad_cross_in = fold(dot(dq2, q2_mine, 0, 1))
    third_pull = jax.vjp(layer_norm, stream_one, rows[10], rows[11])[1]
    from_cross, gain_three, offset_three = third_pull(grad_cross_in)
    grad_one = grad_two + from_cross

    attn_grad = grad_one.astype(BF16)
    bias_out = column_sum(attn_grad)
    attn_grad_all = both(attn_grad)
    grad_attended = dot(out_mine, attn_grad_all, 1, 1).astype(BF16).reshape(LOCAL, HD, -1)
    out_terms = terms_of(attended_turned, attn_grad_all, 0, half_chips)
    qkv_grad, self_sums = self_attention_back(
        raw, grad_attended, logs, norm_columns[:, :4], cosine, sine
    )
    qkv_grad = qkv_grad.reshape(3 * HW, -1)
    grad_attn_in = fold(dot(qkv_grad, qkv_mine, 0, 1))
    qkv_terms = terms_of(attn_turned, qkv_grad, 1, chips)
    first_pull = jax.vjp(layer_norm, stream_zero, rows[3], rows[4])[1]
    from_attn, gain_one, offset_one = first_pull(grad_attn_in)
    grad_zero = grad_one + from_attn
    shift_sum = jnp.sum(grad_attn_in, axis=0, keepdims=True)
    shift_low = (shift_sum + core_swap(shift_sum)).astype(BF16)
    silu_part = dot(shift_low, time_mine, 1, 1)
    silu_grad = ordered(silu_part, core_swap(silu_part), 1)
    grad_temb = jax.vjp(jax.nn.silu, temb)[1](silu_grad)[0]
    device = 2 * chip + core

    skip_pull = jax.vjp(layer_norm, skip_proj, rows[1], rows[2])[1]
    grad_proj, gain_skip, offset_skip = skip_pull(grad_zero)
    proj_low = grad_proj.astype(BF16)
    bias_skip = column_sum(proj_low)
    proj_all = both(proj_low)
    skip_terms = terms_of(joined_turned, proj_all, 0, half_chips)
    proj_late = tie(proj_low, skip_terms)
    grad_hidden = dot(proj_late, hidden_rows, 1, 1)
    grad_skip = dot(proj_late, skipped_rows, 1, 1)

    def split_rows(value, pieces):
        parts = [value[2 * a : 2 * b].reshape(2, b - a, -1) for a, b in zip(pieces, pieces[1:])]
        mine = jnp.concatenate([take(p, core, 0) for p in parts], axis=0)
        other = jnp.concatenate([take(p, 1 - core, 0) for p in parts], axis=0)
        return mine, core_swap(other)

    def column_results(value, pieces, groups=1):
        mine, other = split_rows(value, pieces)
        width = value.shape[1] // groups
        columns = []
        for g in range(groups):
            part = slice(g * width, (g + 1) * width)
            columns += [
                jnp.where(first_core, mine[:, part], other[:, part]),
                jnp.where(first_core, other[:, part], mine[:, part]),
            ]
        whole = jnp.concatenate(columns, axis=1)
        return [whole[a:b] for a, b in zip(pieces, pieces[1:])]

    def row_results(value, pieces):
        mine, other = split_rows(value, pieces)
        whole = jnp.where(own_half, mine, other)
        return [whole[a:b] for a, b in zip(pieces, pieces[1:])]

    one_piece = (0, own_rows)
    two_cuts = (0, own_rows, 2 * own_rows)
    fc1_grad, fc2_grad = scatter_group(
        [(*fc1_terms, orders[0], False), (*fc2_terms, orders[1], False)],
        (dq2, attn_grad, skip_terms, skip_terms),
    )
    (grad_fc1,) = column_results(tie(fc1_grad, skip_terms), one_piece)
    grad_fc2 = column_results(tie(fc2_grad, skip_terms), one_piece)[0].T
    pair_terms = [jnp.concatenate(parts, axis=1) for parts in zip(out_terms, out2_terms)]
    four_grad, pair_grad = scatter_group(
        [(*four_terms, orders[0], False), (*pair_terms, row_orders[1], True)],
        (skip_terms, skip_terms, skip_terms),
    )
    four_results = column_results(four_grad, cuts)
    grad_q2 = four_results[0]
    grad_kv2 = jnp.concatenate(four_results[1:], axis=1)
    grad_out, grad_out2 = row_results(pair_grad, two_cuts)
    (qkv_result,) = scatter_group([(*qkv_terms, orders[0], False)], (skip_terms,))
    (grad_qkv,) = column_results(qkv_result, one_piece, 3)
    (skip_result,) = scatter_group([(*skip_terms, row_orders[1], True)])
    (grad_skipw,) = row_results(skip_result, (0, skip_part))

    def bias_of(grads):
        return spread(column_sum(grads, axis=1).reshape(-1, HW))

    bias_qkv = bias_of(qkv_grad)
    owner = first_core.astype(F32)
    vector_grad = jnp.stack(
        [
            bias_skip,
            gain_skip,
            offset_skip,
            gain_one,
            offset_one,
            shift_low[0].astype(F32) * owner,
            bias_qkv[0],
            bias_qkv[1],
            bias_qkv[2],
            bias_out,
            gain_three,
            offset_three,
            bias_of(dq2)[0],
            bias_of(dk2)[0],
            bias_of(dv2)[0],
            bias_out2,
            gain_two,
            offset_two,
            bias_fc2,
        ]
    )
    norm_grad = jnp.concatenate([jnp.sum(self_sums, axis=2), jnp.sum(cross_sums, axis=2)])
    shift_rows = jnp.where(all_chips[:, None] == chip, shift_low.astype(F32), 0.0) * owner
    packed = jnp.concatenate(
        [x.reshape(-1) for x in (vector_grad, norm_grad, grad_inner_bias, shift_rows)]
    )
    packed = tie(packed, skip_terms)
    packed = packed + core_swap(packed)
    for move in masks_of(chips):
        packed = packed + chip_swap(packed, (move, move))
    vector_count = vector_grad.size
    norm_count = norm_grad.size
    vector_here = vectors.shape[1]
    grad_vectors = lax.dynamic_slice_in_dim(
        packed[:vector_count].reshape(vector_grad.shape), device * vector_here, vector_here, axis=1
    )
    norm_total = packed[vector_count : vector_count + norm_count].reshape(norm_grad.shape)
    bias_end = vector_count + norm_count + hidden_units
    bias_total = packed[vector_count + norm_count : bias_end]
    shift_all = packed[bias_end:].reshape(chips, D).astype(BF16)
    silu_here = lax.dynamic_slice_in_dim(silu_all, device * own_rows, own_rows, axis=1)
    grad_time = dot(silu_here, shift_all, 0, 0)
    return (
        block_out[None],
        grad_hidden[None],
        grad_skip[None],
        grad_text[None],
        grad_temb,
        grad_skipw,
        grad_time,
        grad_qkv,
        grad_out,
        grad_q2,
        grad_kv2,
        grad_out2,
        grad_fc1,
        grad_fc2,
        grad_vectors,
        norm_total,
        bias_total,
    )


def solution(mesh):
    tokens = P("dp", "seq", None)
    rows = P(AXES, None)
    columns = P(None, AXES)
    return jax.shard_map(
        shards,
        mesh=mesh,
        in_specs=(
            tokens,
            tokens,
            P("dp", None, None),
            P("dp", None),
            P("dp"),
            tokens,
            rows,
            rows,
            rows,
            rows,
            rows,
            rows,
            rows,
            rows,
            columns,
            columns,
            P(),
            P(),
        ),
        out_specs=(
            tokens,
            tokens,
            tokens,
            P("dp", None, None),
            P("dp", None),
            rows,
            rows,
            rows,
            rows,
            rows,
            rows,
            rows,
            rows,
            columns,
            columns,
            P(),
            P(),
        ),
        check_vma=False,
    )
```
